256 devices in a mesh: seq: 8 (over y, core), factor: 32 (over z, x).
Axes of the slice: x: 4, y: 4, z: 8, core: 2. Of those that a mesh axis runs over, the one named last changes fastest.
Arguments:
- out_grads: bfloat16 [16384, 28672], P('seq', 'factor'), may hold values from -6 to 6
- in_acts: bfloat16 [16384, 8192], P('seq', 'factor'), may hold values from -6 to 6
- query_grads: bfloat16 [2048, 28672], P('seq', 'factor'), may hold values from -6 to 6
- query_acts: bfloat16 [2048, 8192], P('seq', 'factor'), may hold values from -6 to 6
- output_basis: float32 [1024, 28672], P('factor'), may hold values from -0.03125 to 0.03125
- input_basis: float32 [128, 8192], replicated, may hold values from -0.0625 to 0.0625
- eigenvalues: float32 [1024, 128], P('factor'), may hold values from 0.001 to 50
- doc_ids: int32 [16384], P('seq'), may hold values from 0 to 3, as said below
- doc_lengths: int32 [32], P('seq'), may hold values from 256 to 768, as said below
Outputs:
- scores: float32 [64, 32], P('factor', 'seq')
The draws below stay inside these ranges and needn't reach their ends.
Inputs may be any that keep to these rules, and one draw needn't show every extreme that they name: doc_ids never decrease along the tokens of a group of 2048 consecutive tokens, and document k of group g holds exactly doc_lengths[g * 4 + k] of them. `doc_lengths`: the lengths of each group's 4 documents sum to 2048.
All inputs are finite; a program needn't handle non-finite values.
Results may differ from the reference program's by a relative error of at most 0.0003.
Values sent between devices are 32-bit elements; how exact they have to be, the bound alone decides.
No kernel may reach another device: no remote copies, remote signals or barrier semaphores. Data moves between devices by JAX's collectives and lax.ppermute only.
A program may use at most 64 MiB of HBM per device.

```python
import math
import jax
import jax.numpy as jnp
from jax import lax

D = 8192
FF = 28672
KA = 128
SEQ_DEV = 4
LEN = 512
NQ = 64
QLEN = 32
KG = 1024
DOCS = 32
TOKENS = 16384
QTOKENS = 2048
N_SEQ = 8


def doc_layout(key):
    base = jax.random.fold_in(key, 7)
    pairs = SEQ_DEV // 2

    def group_layout(index):
        group_key = jax.random.fold_in(base, index)
        key_shift, key_order, key_sign = jax.random.split(group_key, 3)
        shift = jax.random.randint(key_shift, (pairs,), 0, LEN // 2 + 1)
        shift = shift.at[0].set(LEN // 2)
        order = jax.random.permutation(key_order, pairs)
        shift = shift[order]
        sign = jax.random.randint(key_sign, (pairs,), 0, 2) * 2 - 1
        lengths = jnp.stack([LEN - sign * shift, LEN + sign * shift], axis=1).reshape(SEQ_DEV)
        ends = jnp.cumsum(lengths)
        position = jnp.arange(SEQ_DEV * LEN)
        member = jnp.sum((position[:, None] >= ends[None, :]).astype(jnp.int32), axis=1)
        return (member.astype(jnp.int32), lengths.astype(jnp.int32))
    member, lengths = jax.vmap(group_layout)(jnp.arange(N_SEQ))
    return (member.reshape(-1), lengths.reshape(-1))


def draw_doc_ids(key, part):
    return doc_layout(key)[0]


def draw_doc_lengths(key, part):
    return doc_layout(key)[1]


def block_levels(own_key, extent, shards, smallest, high):
    gain, own = 1.0, jax.random.fold_in(own_key, 6)
    for axis_at, shards_of in shards:
        draws = jnp.exp(jax.random.uniform(jax.random.fold_in(own, axis_at), (shards_of,), jnp.float32, smallest / len(shards), high / len(shards)))
        gain = gain * jnp.repeat(draws, extent[axis_at] // shards_of).reshape([-1 if axis == axis_at else 1 for axis in range(len(extent))])
    return gain


def scatter_about(rng, extent, scale, limit, cuts=(), kind=jnp.bfloat16):
    entries = scale * jax.random.normal(rng, extent, jnp.float32)
    if cuts:
        entries = entries * block_levels(rng, extent, cuts, -0.22, 0.18)
    return jnp.clip(entries, -limit, limit).astype(kind)


def setup_inputs(seed: int = 0) -> dict:
    key_of = jax.random.split(jax.random.key(seed), 10)
    out_grads = scatter_about(key_of[0], (TOKENS, FF), 1.0, 6.0, ((0, 8), (1, 32)))
    in_acts = scatter_about(key_of[1], (TOKENS, D), 1.0, 6.0, ((0, 8), (1, 32)))
    query_grads = scatter_about(key_of[2], (QTOKENS, FF), 1.0, 6.0, ((0, 8), (1, 32)))
    query_acts = scatter_about(key_of[3], (QTOKENS, D), 1.0, 6.0, ((0, 8), (1, 32)))
    output_basis = scatter_about(key_of[4], (KG, FF), FF ** -0.5, 0.03125, ((0, 32),), jnp.float32)
    input_basis = scatter_about(key_of[5], (KA, D), D ** -0.5, 0.0625, (), jnp.float32)
    eigenvalues = jnp.clip(jnp.exp(math.log(50.0) - 10.819778 * jax.random.uniform(key_of[6], (KG, KA), jnp.float32) ** block_levels(key_of[6], (KG, KA), ((0, 32),), -0.2, 0.2)), 0.001, 50.0)
    doc_ids = draw_doc_ids(jax.random.fold_in(key_of[9], 71), 0)
    doc_lengths = draw_doc_lengths(jax.random.fold_in(key_of[9], 71), 0)
    return {"out_grads": out_grads, "in_acts": in_acts, "query_grads": query_grads, "query_acts": query_acts, "output_basis": output_basis, "input_basis": input_basis, "eigenvalues": eigenvalues, "doc_ids": doc_ids, "doc_lengths": doc_lengths}


DAMPING = 1.0


def rotate_group(gradients, activations, weights, output_basis, input_basis):
    rot_in = jnp.dot(activations.astype(jnp.float32), input_basis.T, precision=lax.Precision.HIGHEST)
    rot_out = jnp.dot(gradients.astype(jnp.float32), output_basis.T, precision=lax.Precision.HIGHEST)
    column_count = weights.shape[1]
    spread = (weights[:, :, None] * rot_in[:, None, :]).reshape(rot_in.shape[0], column_count * KA)
    return jnp.dot(rot_out.T, spread, precision=lax.Precision.HIGHEST)


def reference(out_grads, in_acts, query_grads, query_acts, output_basis, input_basis, eigenvalues, doc_ids, doc_lengths):
    group_tokens = SEQ_DEV * LEN
    group_grads = out_grads.reshape(N_SEQ, group_tokens, FF)
    group_acts = in_acts.reshape(N_SEQ, group_tokens, D)
    membership = doc_ids.reshape(N_SEQ, group_tokens)
    doc_sizes = doc_lengths.reshape(N_SEQ, SEQ_DEV).astype(jnp.float32)
    local_docs = jnp.arange(SEQ_DEV, dtype=jnp.int32)

    def train_group(group_items):
        these_grads, these_acts, these_members, these_sizes = group_items
        weights = (these_members[:, None] == local_docs[None, :]).astype(jnp.float32) / these_sizes[None, :]
        return rotate_group(these_grads, these_acts, weights, output_basis, input_basis)

    train_rot = lax.map(train_group, (group_grads, group_acts, membership, doc_sizes))
    train_rot = train_rot.reshape(N_SEQ, KG, SEQ_DEV, KA)

    per_group = NQ // N_SEQ
    query_tokens = per_group * QLEN
    query_group_grads = query_grads.reshape(N_SEQ, query_tokens, FF)
    query_group_acts = query_acts.reshape(N_SEQ, query_tokens, D)
    query_owner = jnp.arange(query_tokens, dtype=jnp.int32) // QLEN
    query_weights = (query_owner[:, None] == jnp.arange(per_group, dtype=jnp.int32)[None, :]).astype(jnp.float32) / QLEN

    def query_group(group_items):
        these_grads, these_acts = group_items
        return rotate_group(these_grads, these_acts, query_weights, output_basis, input_basis)

    query_rot = lax.map(query_group, (query_group_grads, query_group_acts))
    query_rot = query_rot.reshape(N_SEQ, KG, per_group, KA)
    query_rot = jnp.transpose(query_rot, (1, 0, 2, 3)).reshape(KG, NQ, KA)
    precond = query_rot / (eigenvalues[:, None, :] + DAMPING)
    scores = jnp.einsum('kqj,gkdj->qgd', precond, train_rot, precision=lax.Precision.HIGHEST)
    return scores.reshape(NQ, DOCS)
```

```python
import jax
import jax.numpy as jnp
from jax import lax
from jax.sharding import Mesh, PartitionSpec as P

QLEN = 32
DAMPING = 1.0
ZX = ("z", "x")
HIGH = lax.Precision.HIGH
HIGHEST = lax.Precision.HIGHEST


def exchange(blocks, axis):
    return lax.all_to_all(blocks, axis, 0, 0, tiled=True)


def gathered(shard, axis):
    return exchange(jnp.broadcast_to(shard[None], (lax.axis_size(axis), *shard.shape)), axis)


def from_ahead(shard, axis, hops):
    n = lax.axis_size(axis)
    return lax.ppermute(shard, axis, [((i + hops) % n, i) for i in range(n)])


def dot(left, right, left_dim, right_dim, precision):
    return lax.dot_general(
        left,
        right,
        (((left_dim,), (right_dim,)), ((), ())),
        precision=precision,
        preferred_element_type=jnp.float32,
    )


def reduced_over_x(slabs):
    n = slabs.shape[-1]
    blocks = jnp.moveaxis(slabs, 1, 0).reshape(4, 256, n)
    summed = jnp.sum(exchange(blocks, "x"), axis=0)
    return jnp.moveaxis(summed.reshape(8, 8, 4, n), 1, 0).reshape(8, 32, n)


def local(
    out_grads,
    in_acts,
    query_grads,
    query_acts,
    output_basis,
    input_basis,
    eigenvalues,
    doc_ids,
    doc_lengths,
):
    y, core = lax.axis_index("y"), lax.axis_index("core")
    seq = 2 * y + core
    factor = 4 * lax.axis_index("z") + lax.axis_index("x")
    width = in_acts.shape[1]
    tokens, query_tokens = in_acts.shape[0], query_acts.shape[0]

    basis_part = lax.dynamic_slice_in_dim(input_basis, factor * width, width, 1)
    partial = jnp.concatenate(
        [dot(in_acts, basis_part, 1, 1, HIGH), dot(query_acts, basis_part, 1, 1, HIGH)], 0
    )
    inner = partial.shape[1]
    rows = partial.shape[0]
    part = jnp.sum(exchange(partial.reshape(4, rows // 4, inner), "x"), axis=0)
    part = jnp.sum(exchange(part.reshape(8, rows // 32, inner), "z"), axis=0)
    part = gathered(part, "z").reshape(rows // 4, inner)
    rot_in = gathered(part, "x").reshape(rows, inner)
    rot_train, rot_query = rot_in[:tokens], rot_in[tokens:]

    cols = output_basis.shape[1] // 32
    mine = lax.dynamic_slice_in_dim(output_basis, 4 * seq, 4, 0)
    got = exchange(jnp.moveaxis(mine.reshape(4, 32, cols), 1, 0), ZX)
    own = jnp.moveaxis(got.reshape(8, 4, 4, cols), 1, 0).reshape(128, cols)
    slabs = jnp.stack([own] + [from_ahead(own, "y", k) for k in (1, 2, 3)])
    other = from_ahead(slabs, "core", 1)
    basis_cols = jnp.concatenate([slabs, other], 0).reshape(1024, cols)

    slot = jnp.arange(32, dtype=jnp.int32)
    slot_seq = 2 * ((y + (slot // 4) % 4) % 4) + (core + slot // 16) % 2
    place = 4 * slot_seq + slot % 4
    to_order = (slot[:, None] == place[None, :]).astype(jnp.float32)

    query_count = query_tokens // QLEN
    rot = dot(basis_cols, query_grads, 1, 1, HIGH).reshape(8, 4, 8, 4, query_tokens)
    rot = jnp.sum(exchange(reduced_over_x(rot), "z"), axis=0)
    rot = dot(to_order, rot, 1, 0, HIGHEST)
    query_rot = jnp.einsum(
        "kqt,qtj->kqj",
        rot.reshape(32, query_count, QLEN),
        rot_query.reshape(query_count, QLEN, inner),
        precision=HIGHEST,
    ) * (1.0 / QLEN)
    precond = query_rot / (eigenvalues[:, None, :] + DAMPING)
    precond = gathered(precond, "y")
    precond = gathered(precond, "core")

    doc_count = doc_lengths.shape[0]
    local_docs = jnp.arange(doc_count, dtype=jnp.int32)
    weights = (doc_ids[:, None] == local_docs[None, :]).astype(jnp.float32) / doc_lengths.astype(
        jnp.float32
    )[None, :]
    spread = (weights[:, :, None] * rot_train[:, None, :]).reshape(tokens, doc_count * inner)
    summed = dot(out_grads, spread, 0, 0, HIGH)
    train = jnp.dot(basis_cols, summed, precision=HIGH).reshape(8, 4, 8, 4, doc_count * inner)
    train = jnp.sum(exchange(reduced_over_x(train), "z"), axis=0)
    train = dot(to_order, train, 1, 0, HIGHEST).reshape(32, doc_count, inner)

    partial_scores = jnp.einsum("cykqj,kdj->ycqd", precond, train, precision=HIGHEST)
    partial_scores = partial_scores.reshape(32, 2, doc_count)
    return jnp.sum(exchange(partial_scores, ZX), axis=0)


def solution(mesh):
    fine = Mesh(mesh.devices.reshape(4, 2, 8, 4), ("y", "core", "z", "x"))
    seq, factor = ("y", "core"), ("z", "x")
    in_specs = (
        P(seq, factor),
        P(seq, factor),
        P(seq, factor),
        P(seq, factor),
        P(factor, None),
        P(),
        P(factor, None),
        P(seq),
        P(seq),
    )
    return jax.shard_map(
        local, mesh=fine, in_specs=in_specs, out_specs=P(factor, seq), check_vma=False
    )
```

```python
import functools

import jax
import jax.numpy as jnp
from jax import lax
from jax.experimental import pallas as pl
from jax.experimental.pallas import tpu as pltpu
from jax.sharding import Mesh, PartitionSpec as P

QLEN = 32
DAMPING = 1.0
ZX = ("z", "x")

HALF = 512
VMEM = pl.BlockSpec(memory_space=pltpu.VMEM)
SMEM = pl.BlockSpec(memory_space=pltpu.SMEM)


def exchange(blocks, axis):
    return lax.all_to_all(blocks, axis, 0, 0, tiled=True)


def shifted(shard, axis, hops):
    n = lax.axis_size(axis)
    return lax.ppermute(shard, axis, [(i, (i + hops) % n) for i in range(n)])


def call(kernel, outs, in_specs, *args, scratch=()):
    out_shape = [jax.ShapeDtypeStruct(*o) for o in outs]
    return pl.pallas_call(
        kernel,
        out_shape=out_shape,
        in_specs=in_specs,
        out_specs=[VMEM] * len(out_shape),
        scratch_shapes=list(scratch),
    )(*args)


def place(me_ref):
    me = me_ref[0]
    return me // 64, (me // 32) % 2, (me // 4) % 8, me % 4


def split(value):
    high = value.astype(jnp.bfloat16)
    return high, (value - high.astype(jnp.float32)).astype(jnp.bfloat16)


def dot_nt(left, right):
    return lax.dot_general(
        left, right, (((1,), (1,)), ((), ())), preferred_element_type=jnp.float32
    )


def dot_nn(left, right):
    return lax.dot_general(
        left, right, (((1,), (0,)), ((), ())), preferred_element_type=jnp.float32
    )


def input_rotation_kernel(me_ref, acts_ref, query_ref, basis_ref, *out_refs):
    _, _, z, x = place(me_ref)
    width = acts_ref.shape[1]
    start = pl.multiple_of((4 * z + x) * width, width)
    high, low = split(basis_ref[:, pl.ds(start, width)])
    for k, out_ref in enumerate(out_refs):
        target = lax.rem(x + k, 4)
        acts = acts_ref[pl.ds(pl.multiple_of(target * 512, 512), 512), :]
        query = query_ref[pl.ds(pl.multiple_of(target * 64, 64), 64), :]
        out_ref[:, :64, :] = (dot_nt(acts, high) + dot_nt(acts, low)).reshape(8, 64, 128)
        out_ref[:, 64:, :] = (dot_nt(query, high) + dot_nt(query, low)).reshape(8, 8, 128)


def basis_pick_kernel(me_ref, basis_ref, out_ref):
    y, core, _, _ = place(me_ref)
    cols = basis_ref.shape[1] // 32
    rows = pl.ds(pl.multiple_of(8 * y, 8), 8)
    for f in range(32):
        start = pl.multiple_of(f * cols + core * (cols - HALF), 128)
        out_ref[f] = basis_ref[rows, pl.ds(start, HALF)]


def query_kernel(me_ref, grads_ref, *refs):
    slabs, out_ref, halves_ref = refs[:8], refs[8], refs[9]
    _, core, _, _ = place(me_ref)
    cols = grads_ref.shape[1]
    halves_ref[0] = grads_ref[:, :HALF]
    halves_ref[1, :, : 2 * HALF - cols] = jnp.zeros((grads_ref.shape[0], 2 * HALF - cols), jnp.bfloat16)
    halves_ref[1, :, 2 * HALF - cols :] = grads_ref[:, HALF:]
    own, other = halves_ref[core], halves_ref[1 - core]
    for slot in range(4):
        total = None
        for half, ref in ((own, slabs[slot]), (other, slabs[4 + slot])):
            high, low = split(ref[...].reshape(256, HALF))
            part = dot_nt(high, half) + dot_nt(low, half)
            total = part if total is None else total + part
        out_ref[:, :, slot] = total.reshape(8, 4, 8, total.shape[1])


def query_sum_kernel(me_ref, blocks_ref, *out_refs):
    _, _, _, x = place(me_ref)
    for k, out_ref in enumerate(out_refs):
        target = lax.rem(x + k, 4)
        total = blocks_ref[0, target]
        for sender in range(1, 8):
            total = total + blocks_ref[sender, target]
        out_ref[...] = total


def precond_kernel(me_ref, eig_ref, *refs):
    parts, blocks, out_ref, rot_in_ref = refs[:4], refs[4:8], refs[8], refs[9]
    y, _, _, x = place(me_ref)
    for k in range(4):
        source = lax.rem(x + 4 - k, 4)
        rot_in_ref[pl.ds(pl.multiple_of(source * 64, 64), 64), :] = blocks[k][:, 64:, :].reshape(64, 128)
    rot = parts[0][...] + parts[1][...] + parts[2][...] + parts[3][...]
    rot = rot.reshape(32, rot.shape[-1])
    lane_query = lax.broadcasted_iota(jnp.int32, rot.shape, 1) // QLEN
    count = rot.shape[1] // QLEN
    masked = jnp.concatenate([jnp.where(lane_query == q, rot, 0.0) for q in range(count)], 0)
    both = lax.dot_general(
        masked,
        rot_in_ref[...],
        (((1,), (0,)), ((), ())),
        precision=lax.Precision.HIGHEST,
        preferred_element_type=jnp.float32,
    ) * (1.0 / QLEN)
    for slot in range(4):
        rows = pl.ds(pl.multiple_of(8 * lax.rem(y + slot, 4), 8), 8)
        eig = eig_ref[rows, :] + DAMPING
        for q in range(count):
            out_ref[rows, q, :] = both[32 * q + 8 * slot : 32 * q + 8 * slot + 8] / eig


def outer_sum_kernel(me_ref, len_ref, grads_ref, *refs):
    blocks, (high_ref, low_ref, total_ref) = refs[:4], refs[4:]
    _, _, _, x = place(me_ref)
    cols = grads_ref.shape[1]
    total_ref[...] = jnp.zeros_like(total_ref)
    for k in range(4):
        source = lax.rem(x + 4 - k, 4)
        first = pl.multiple_of(source * 512, 512)
        grads = grads_ref[pl.ds(first, 512), :]
        high, low = split(blocks[k][:, :64, :].reshape(512, 128).T)
        pair = jnp.concatenate([high, low], 0)
        token = first + lax.broadcasted_iota(jnp.int32, pair.shape, 1)
        begin = jnp.int32(0)
        for doc in range(4):
            end = begin + len_ref[doc]

            @pl.when((begin < first + 512) & (end > first))
            def _(begin=begin, end=end, doc=doc, pair=pair, token=token, grads=grads):
                masked = jnp.where((token >= begin) & (token < end), pair, jnp.zeros_like(pair))
                both = dot_nn(masked, grads)
                total_ref[doc] += both[:128] + both[128:]

            begin = end
    for doc in range(4):
        length = jnp.full((128, cols), len_ref[doc], jnp.int32).astype(jnp.float32)
        high, low = split(total_ref[doc] / length)
        rows = slice(128 * doc, 128 * doc + 128)
        for ref, value in ((high_ref, high), (low_ref, low)):
            ref[0, rows, :] = value[:, :HALF]
            ref[1, rows, : 2 * HALF - cols] = jnp.zeros((128, 2 * HALF - cols), jnp.bfloat16)
            ref[1, rows, 2 * HALF - cols :] = value[:, HALF:]


def train_kernel(hops, me_ref, high_ref, low_ref, *refs):
    slabs, out_refs = refs[:8], refs[8:]
    _, core, _, x = place(me_ref)
    for k, out_ref in zip(hops, out_refs):
        target = lax.rem(x + k, 4)
        total = None
        for half, group in ((core, slabs[:4]), (1 - core, slabs[4:])):
            value = jnp.concatenate([ref[:, target].reshape(64, HALF) for ref in group], 0)
            high, low = split(value)
            part = dot_nt(high, high_ref[half]) + dot_nt(high, low_ref[half]) + dot_nt(low, high_ref[half])
            total = part if total is None else total + part
        for slot in range(4):
            out_ref[:, 8 * slot : 8 * slot + 8, :] = total[64 * slot : 64 * slot + 64].reshape(8, 8, 512)


def score_kernel(me_ref, blocks_ref, *refs):
    preconds, out_ref = refs[:8], refs[8]
    y, core, _, _ = place(me_ref)
    train = blocks_ref[0]
    for sender in range(1, 8):
        train = train + blocks_ref[sender]
    for index, ref in enumerate(preconds):
        other, k = divmod(index, 4)
        owner = 2 * lax.rem(y + 4 - k, 4) + lax.rem(core + other, 2)
        sums = [None] * 4
        for slot in range(4):
            base = 8 * lax.rem(y + slot, 4)
            for r in range(8):
                value = ref[base + r]
                row = train[8 * slot + r : 8 * slot + r + 1]
                for doc in range(4):
                    product = value * row[:, 128 * doc : 128 * doc + 128]
                    sums[doc] = product if sums[doc] is None else sums[doc] + product
        for q in range(8):
            for doc in range(4):
                out_ref[4 * owner + q // 2, 4 * (q % 2) + doc : 4 * (q % 2) + doc + 1, :] = sums[doc][q : q + 1]


def local(
    out_grads,
    in_acts,
    query_grads,
    query_acts,
    output_basis,
    input_basis,
    eigenvalues,
    doc_ids,
    doc_lengths,
):
    f32, bf16 = jnp.float32, jnp.bfloat16
    me = lax.axis_index(("y", "core", "z", "x")).astype(jnp.int32).reshape(1)

    parts = call(
        input_rotation_kernel,
        [((8, 72, 128), f32)] * 4,
        [SMEM, VMEM, VMEM, VMEM],
        me, in_acts, query_acts, input_basis,
    )
    part = parts[0] + shifted(parts[1], "x", 1) + shifted(parts[2], "x", 2) + shifted(parts[3], "x", 3)
    part = jnp.sum(exchange(part, "z"), axis=0)
    block = exchange(jnp.broadcast_to(part[None], (8, 72, 128)), "z")
    blocks = [block] + [shifted(block, "x", k) for k in (1, 2, 3)]

    (picked,) = call(basis_pick_kernel, [((32, 8, HALF), f32)], [SMEM, VMEM], me, output_basis)
    slab = exchange(picked, ZX).reshape(8, 4, 8, HALF)
    slabs = [slab] + [shifted(slab, "y", 4 - k) for k in (1, 2, 3)]
    slabs = slabs + [shifted(s, "core", 1) for s in slabs]

    (rot,) = call(
        query_kernel,
        [((8, 4, 4, 8, query_grads.shape[0]), f32)],
        [SMEM] + [VMEM] * 9,
        me, query_grads, *slabs,
        scratch=[pltpu.VMEM((2, query_grads.shape[0], HALF), bf16)],
    )
    rots = call(
        query_sum_kernel,
        [((4, 8, query_grads.shape[0]), f32)] * 4,
        [SMEM, VMEM],
        me, exchange(rot, "z"),
    )
    rots = [rots[0]] + [shifted(rots[k], "x", k) for k in (1, 2, 3)]
    (precond,) = call(
        precond_kernel,
        [((32, 8, 128), f32)],
        [SMEM] + [VMEM] * 9,
        me, eigenvalues, *rots, *blocks,
        scratch=[pltpu.VMEM((query_grads.shape[0], 128), f32)],
    )
    preconds = [precond] + [shifted(precond, "y", k) for k in (1, 2, 3)]
    preconds = preconds + [shifted(p, "core", 1) for p in preconds]

    high, low = call(
        outer_sum_kernel,
        [((2, 512, HALF), bf16)] * 2,
        [SMEM, SMEM] + [VMEM] * 5,
        me, doc_lengths, out_grads, *blocks,
        scratch=[pltpu.VMEM((4, 128, out_grads.shape[1]), f32)],
    )
    train_shape = ((8, 32, 512), f32)
    train_specs = [SMEM] + [VMEM] * 10
    sent = call(functools.partial(train_kernel, (2, 1, 3)), [train_shape] * 3, train_specs, me, high, low, *slabs)
    (kept,) = call(functools.partial(train_kernel, (0,)), [train_shape], train_specs, me, high, low, *slabs)
    train = kept + shifted(sent[0], "x", 2) + shifted(sent[1], "x", 1) + shifted(sent[2], "x", 3)
    train = exchange(train, "z")

    (partial_scores,) = call(
        score_kernel,
        [((32, 8, 128), f32)],
        [SMEM] + [VMEM] * 9,
        me, train, *preconds,
    )
    return jnp.sum(exchange(partial_scores, ZX), axis=(0, 2)).reshape(2, 4)


def solution(mesh):
    fine = Mesh(mesh.devices.reshape(4, 2, 8, 4), ("y", "core", "z", "x"))
    seq, factor = ("y", "core"), ("z", "x")
    in_specs = (
        P(seq, factor),
        P(seq, factor),
        P(seq, factor),
        P(seq, factor),
        P(factor, None),
        P(),
        P(factor, None),
        P(seq),
        P(seq),
    )
    return jax.shard_map(
        local, mesh=fine, in_specs=in_specs, out_specs=P(factor, seq), check_vma=False
    )
```

```python
import jax
import jax.numpy as jnp
from jax import lax
from jax.experimental import pallas as pl
from jax.experimental.pallas import tpu as pltpu
from jax.sharding import Mesh, PartitionSpec as P


QLEN = 32
DAMPING = 1.0
ZX = ("z", "x")

HALF = 512
VMEM = pl.BlockSpec(memory_space=pltpu.VMEM)
SMEM = pl.BlockSpec(memory_space=pltpu.SMEM)


def exchange(blocks, axis):
    return lax.all_to_all(blocks, axis, 0, 0, tiled=True)


def shifted(shard, axis, hops):
    n = lax.axis_size(axis)
    return lax.ppermute(shard, axis, [(i, (i + hops) % n) for i in range(n)])


def call(kernel, outs, in_specs, me, *args, grid=1, scratch=()):
    out_shape = [jax.ShapeDtypeStruct(*o) for o in outs]
    return pl.pallas_call(
        kernel,
        out_shape=out_shape,
        grid_spec=pltpu.PrefetchScalarGridSpec(
            num_scalar_prefetch=1,
            grid=(grid,),
            in_specs=in_specs,
            out_specs=[VMEM] * len(out_shape),
            scratch_shapes=list(scratch),
        ),
    )(me, *args)


def place(me_ref):
    me = me_ref[0]
    return me // 64, (me // 32) % 2, (me // 4) % 8, me % 4


def split(value):
    high = value.astype(jnp.bfloat16)
    return high, (value - high.astype(jnp.float32)).astype(jnp.bfloat16)


def dot_nt(left, right):
    return lax.dot_general(
        left, right, (((1,), (1,)), ((), ())), preferred_element_type=jnp.float32
    )


def dot_nn(left, right):
    return lax.dot_general(
        left, right, (((1,), (0,)), ((), ())), preferred_element_type=jnp.float32
    )


def input_rotation_kernel(me_ref, acts_ref, query_ref, basis_ref, *out_refs):
    _, _, _, x = place(me_ref)
    high, low = split(basis_ref[...])
    for k, out_ref in enumerate(out_refs):
        target = lax.rem(x + k, 4)
        acts = acts_ref[pl.ds(pl.multiple_of(target * 512, 512), 512), :]
        query = query_ref[pl.ds(pl.multiple_of(target * 64, 64), 64), :]
        out_ref[:, :64, :] = (dot_nt(acts, high) + dot_nt(acts, low)).reshape(8, 64, 128)
        out_ref[:, 64:, :] = (dot_nt(query, high) + dot_nt(query, low)).reshape(8, 8, 128)


def basis_pick_kernel(me_ref, basis_ref, out_ref):
    _, core, _, _ = place(me_ref)
    cols = basis_ref.shape[1] // 32
    for f in range(32):
        start = pl.multiple_of(f * cols + core * (cols - HALF), 128)
        out_ref[f] = basis_ref[:, pl.ds(start, HALF)]


def query_kernel(me_ref, grads_ref, *refs):
    slabs, out_ref, halves_ref = refs[:8], refs[8], refs[9]
    _, core, _, _ = place(me_ref)
    cols = grads_ref.shape[1]
    halves_ref[0] = grads_ref[:, :HALF]
    halves_ref[1, :, : 2 * HALF - cols] = jnp.zeros((grads_ref.shape[0], 2 * HALF - cols), jnp.bfloat16)
    halves_ref[1, :, 2 * HALF - cols :] = grads_ref[:, HALF:]
    own, other = halves_ref[core], halves_ref[1 - core]
    for slot in range(4):
        total = None
        for half, ref in ((own, slabs[slot]), (other, slabs[4 + slot])):
            high, low = split(ref[...].reshape(256, HALF))
            part = dot_nt(high, half) + dot_nt(low, half)
            total = part if total is None else total + part
        out_ref[:, :, slot] = total.reshape(8, 4, 8, total.shape[1])


def query_sum_kernel(me_ref, blocks_ref, *out_refs):
    _, _, _, x = place(me_ref)
    for k, out_ref in enumerate(out_refs):
        target = lax.rem(x + k, 4)
        total = blocks_ref[0, target]
        for sender in range(1, 8):
            total = total + blocks_ref[sender, target]
        out_ref[...] = total


def precond_kernel(me_ref, eig_ref, *refs):
    parts, blocks, out_ref, rot_in_ref = refs[:4], refs[4:8], refs[8], refs[9]
    y, _, _, x = place(me_ref)
    for k in range(4):
        source = lax.rem(x + 4 - k, 4)
        rot_in_ref[pl.ds(pl.multiple_of(source * 64, 64), 64), :] = blocks[k][:, 64:, :].reshape(64, 128)
    rot = parts[0][...] + parts[1][...] + parts[2][...] + parts[3][...]
    rot = rot.reshape(32, rot.shape[-1])
    lane_query = lax.broadcasted_iota(jnp.int32, rot.shape, 1) // QLEN
    count = rot.shape[1] // QLEN
    masked = jnp.concatenate([jnp.where(lane_query == q, rot, 0.0) for q in range(count)], 0)
    both = lax.dot_general(
        masked,
        rot_in_ref[...],
        (((1,), (0,)), ((), ())),
        precision=lax.Precision.HIGHEST,
        preferred_element_type=jnp.float32,
    ) * (1.0 / QLEN)
    for slot in range(4):
        rows = pl.ds(pl.multiple_of(8 * lax.rem(y + slot, 4), 8), 8)
        eig = eig_ref[rows, :] + DAMPING
        for q in range(count):
            out_ref[rows, q, :] = both[32 * q + 8 * slot : 32 * q + 8 * slot + 8] / eig


def hops_of(step):
    return jnp.where(step < 3, 2 + (step == 2).astype(jnp.int32) - (step == 1).astype(jnp.int32), 0)


def train_kernel(me_ref, len_ref, grads_ref, *refs):
    blocks, slabs, out_refs, (high_ref, low_ref, total_ref) = refs[:4], refs[4:12], refs[12:16], refs[16:]
    _, core, _, x = place(me_ref)
    step = pl.program_id(0)
    cols = grads_ref.shape[1]

    @pl.when(step == 0)
    def _():
        total_ref[...] = jnp.zeros_like(total_ref)

    for k in range(4):

        @pl.when(step == k)
        def _(k=k):
            first = lax.rem(x + 4 - k, 4) * 512
            high, low = split(blocks[k][:, :64, :].reshape(512, 128).T)
            pair = jnp.concatenate([high, low], 0)
            token = first + lax.broadcasted_iota(jnp.int32, pair.shape, 1)
            begin = jnp.int32(0)
            for doc in range(4):
                end = begin + len_ref[doc]

                @pl.when((begin < first + 512) & (end > first))
                def _(begin=begin, end=end, doc=doc):
                    masked = jnp.where((token >= begin) & (token < end), pair, jnp.zeros_like(pair))
                    both = dot_nn(masked, grads_ref[...])
                    total_ref[doc] += both[:128] + both[128:]

                begin = end

    @pl.when(step == 3)
    def _():
        for doc in range(4):
            length = jnp.full((128, cols), len_ref[doc], jnp.int32).astype(jnp.float32)
            high, low = split(total_ref[doc] / length)
            rows = slice(128 * doc, 128 * doc + 128)
            for ref, value in ((high_ref, high), (low_ref, low)):
                ref[0, rows, :] = value[:, :HALF]
                ref[1, rows, : 2 * HALF - cols] = jnp.zeros((128, 2 * HALF - cols), jnp.bfloat16)
                ref[1, rows, 2 * HALF - cols :] = value[:, HALF:]

    @pl.when(step >= 4)
    def _():
        total = None
        for half, group in ((core, slabs[:4]), (1 - core, slabs[4:])):
            value = jnp.concatenate([ref[...].reshape(64, HALF) for ref in group], 0)
            high, low = split(value)
            part = dot_nt(high, high_ref[half]) + dot_nt(high, low_ref[half]) + dot_nt(low, high_ref[half])
            total = part if total is None else total + part
        for at, out_ref in zip((4, 5, 6, 7), out_refs):

            @pl.when(step == at)
            def _(out_ref=out_ref):
                for slot in range(4):
                    out_ref[:, 8 * slot : 8 * slot + 8, :] = total[64 * slot : 64 * slot + 64].reshape(8, 8, 512)


def score_kernel(me_ref, blocks_ref, *refs):
    preconds, out_ref = refs[:8], refs[8]
    y, core, _, _ = place(me_ref)
    train = blocks_ref[0]
    for sender in range(1, 8):
        train = train + blocks_ref[sender]
    for index, ref in enumerate(preconds):
        other, k = divmod(index, 4)
        owner = 2 * lax.rem(y + 4 - k, 4) + lax.rem(core + other, 2)
        sums = [None] * 4
        for slot in range(4):
            base = 8 * lax.rem(y + slot, 4)
            for r in range(8):
                value = ref[base + r]
                row = train[8 * slot + r : 8 * slot + r + 1]
                for doc in range(4):
                    product = value * row[:, 128 * doc : 128 * doc + 128]
                    sums[doc] = product if sums[doc] is None else sums[doc] + product
        for q in range(8):
            for doc in range(4):
                out_ref[4 * owner + q // 2, 4 * (q % 2) + doc : 4 * (q % 2) + doc + 1, :] = sums[doc][q : q + 1]


def local(
    out_grads,
    in_acts,
    query_grads,
    query_acts,
    output_basis,
    input_basis,
    eigenvalues,
    doc_ids,
    doc_lengths,
):
    f32, bf16 = jnp.float32, jnp.bfloat16
    me = lax.axis_index(("y", "core", "z", "x")).astype(jnp.int32).reshape(1)
    queries = query_grads.shape[0]

    parts = call(
        input_rotation_kernel,
        [((8, 72, 128), f32)] * 4,
        [VMEM, VMEM, pl.BlockSpec((128, in_acts.shape[1]), lambda i, me: (0, me[0] % 32))],
        me, in_acts, query_acts, input_basis,
    )
    arrived = [parts[0]]
    for k in (2, 1, 3):
        arrived.append(shifted(parts[k], "x", k))
    part = arrived[0] + arrived[1] + arrived[2] + arrived[3]
    part = jnp.sum(exchange(part, "z"), axis=0)
    block = exchange(jnp.broadcast_to(part[None], (8, 72, 128)), "z")
    blocks = [block] + [None] * 3
    for k in (2, 1, 3):
        blocks[k] = shifted(block, "x", k)

    (picked,) = call(
        basis_pick_kernel,
        [((32, 8, HALF), f32)],
        [pl.BlockSpec((8, output_basis.shape[1]), lambda i, me: (me[0] // 64, 0))],
        me, output_basis,
    )
    slab = exchange(picked, ZX).reshape(8, 4, 8, HALF)
    slabs = [slab] + [shifted(slab, "y", 4 - k) for k in (1, 2, 3)]
    slabs = slabs + [shifted(s, "core", 1) for s in slabs]

    (rot,) = call(
        query_kernel,
        [((8, 4, 4, 8, queries), f32)],
        [VMEM] * 9,
        me, query_grads, *slabs,
        scratch=[pltpu.VMEM((2, queries, HALF), bf16)],
    )
    rot = exchange(rot, "z")
    rots = call(query_sum_kernel, [((4, 8, queries), f32)] * 4, [VMEM], me, rot)
    rots = [rots[0]] + [shifted(rots[k], "x", k) for k in (1, 2, 3)]
    (precond,) = call(
        precond_kernel,
        [((32, 8, 128), f32)],
        [VMEM] * 9,
        me, eigenvalues, *rots, *blocks,
        scratch=[pltpu.VMEM((queries, 128), f32)],
    )
    preconds = [precond]
    for k in (1, 2, 3):
        preconds.append(shifted(precond, "y", k))
    preconds = preconds + [shifted(p, "core", 1) for p in preconds]

    def slab_index(step, me):
        return (0, lax.rem(me[0] % 4 + hops_of(jnp.maximum(step - 4, 0)), 4), 0, 0)

    sent = call(
        train_kernel,
        [((8, 32, 512), f32)] * 4,
        [
            SMEM,
            pl.BlockSpec((512, out_grads.shape[1]), lambda i, me: (lax.rem(me[0] % 4 + 4 - jnp.minimum(i, 3), 4), 0)),
            *[VMEM] * 4,
            *[pl.BlockSpec((8, 1, 8, HALF), slab_index)] * 8,
        ],
        me, doc_lengths, out_grads, *blocks, *slabs,
        grid=8,
        scratch=[
            pltpu.VMEM((2, 512, HALF), bf16),
            pltpu.VMEM((2, 512, HALF), bf16),
            pltpu.VMEM((4, 128, out_grads.shape[1]), f32),
        ],
    )
    arrived = [sent[3]]
    for n, k in enumerate((2, 1, 3)):
        arrived.append(shifted(sent[n], "x", k))
    train = arrived[0] + arrived[1] + arrived[2] + arrived[3]
    train = exchange(train, "z")

    (partial_scores,) = call(score_kernel, [((32, 8, 128), f32)], [VMEM] * 9, me, train, *preconds)
    return jnp.sum(exchange(partial_scores, ZX), axis=(0, 2)).reshape(2, 4)


def solution(mesh):
    fine = Mesh(mesh.devices.reshape(4, 2, 8, 4), ("y", "core", "z", "x"))
    seq, factor = ("y", "core"), ("z", "x")
    in_specs = (
        P(seq, factor),
        P(seq, factor),
        P(seq, factor),
        P(seq, factor),
        P(factor, None),
        P(),
        P(factor, None),
        P(seq),
        P(seq),
    )

    return jax.shard_map(local, mesh=fine, in_specs=in_specs, out_specs=P(factor, seq), check_vma=False)
```

```python
import functools

import jax
import jax.numpy as jnp
from jax import lax
from jax.experimental import pallas as pl
from jax.experimental.pallas import tpu as pltpu
from jax.sharding import Mesh, PartitionSpec as P


QLEN = 32
DAMPING = 1.0
ZX = ("z", "x")

HALF = 512
VMEM = pl.BlockSpec(memory_space=pltpu.VMEM)
SMEM = pl.BlockSpec(memory_space=pltpu.SMEM)


def exchange(blocks, axis):
    return lax.all_to_all(blocks, axis, 0, 0, tiled=True)


def shifted(shard, axis, hops):
    n = lax.axis_size(axis)
    return lax.ppermute(shard, axis, [(i, (i + hops) % n) for i in range(n)])


def call(kernel, outs, in_specs, me, *, args, grid=1, scratch=()):
    out_shape = [jax.ShapeDtypeStruct(*o) for o in outs]
    return pl.pallas_call(
        kernel,
        out_shape=out_shape,
        grid_spec=pltpu.PrefetchScalarGridSpec(
            num_scalar_prefetch=1,
            grid=(grid,),
            in_specs=in_specs,
            out_specs=[VMEM] * len(out_shape),
            scratch_shapes=list(scratch),
        ),
    )(me, *args)


def place(me_ref):
    me = me_ref[0]
    return me // 64, (me // 32) % 2, (me // 4) % 8, me % 4


def split(value):
    high = value.astype(jnp.bfloat16)
    return high, (value - high.astype(jnp.float32)).astype(jnp.bfloat16)


def dot_nt(left, right):
    return lax.dot_general(
        left, right, (((1,), (1,)), ((), ())), preferred_element_type=jnp.float32
    )


def dot_nn(left, right):
    return lax.dot_general(
        left, right, (((1,), (0,)), ((), ())), preferred_element_type=jnp.float32
    )


def input_rotation_kernel(me_ref, acts_ref, query_ref, basis_ref, *out_refs):
    _, _, _, x = place(me_ref)
    high, low = split(basis_ref[...])
    for k, out_ref in enumerate(out_refs):
        target = lax.rem(x + k, 4)
        acts = acts_ref[pl.ds(pl.multiple_of(target * 512, 512), 512), :]
        query = query_ref[pl.ds(pl.multiple_of(target * 64, 64), 64), :]
        out_ref[:, :64, :] = (dot_nt(acts, high) + dot_nt(acts, low)).reshape(8, 64, 128)
        out_ref[:, 64:, :] = (dot_nt(query, high) + dot_nt(query, low)).reshape(8, 8, 128)


def basis_pick_kernel(me_ref, basis_ref, out_ref):
    _, core, _, _ = place(me_ref)
    cols = basis_ref.shape[1] // 32
    for f in range(32):
        start = pl.multiple_of(f * cols + core * (cols - HALF), 128)
        out_ref[f] = basis_ref[:, pl.ds(start, HALF)]


def block_sum_kernel(me_ref, blocks_ref, out_ref):
    total = blocks_ref[0]
    for sender in range(1, 8):
        total = total + blocks_ref[sender]
    for target in range(8):
        out_ref[target] = total


def query_kernel(own, me_ref, grads_ref, *refs):
    so_far = None if own else refs[0]
    slabs, out_ref, half_ref = refs[-6:-2], refs[-2], refs[-1]
    _, core, _, _ = place(me_ref)
    cols = grads_ref.shape[1]
    half = core if own else 1 - core

    @pl.when(half == 0)
    def _():
        half_ref[...] = grads_ref[:, :HALF]

    @pl.when(half == 1)
    def _():
        half_ref[:, : 2 * HALF - cols] = jnp.zeros((grads_ref.shape[0], 2 * HALF - cols), jnp.bfloat16)
        half_ref[:, 2 * HALF - cols :] = grads_ref[:, HALF:]

    for slot in range(4):
        high, low = split(slabs[slot][...].reshape(256, HALF))
        total = (dot_nt(high, half_ref[...]) + dot_nt(low, half_ref[...])).reshape(8, 4, 8, half_ref.shape[0])
        out_ref[:, :, slot] = total if own else so_far[:, :, slot] + total


def query_sum_kernel(me_ref, blocks_ref, *out_refs):
    _, _, _, x = place(me_ref)
    for k, out_ref in enumerate(out_refs):
        target = lax.rem(x + k, 4)
        total = blocks_ref[0, target]
        for sender in range(1, 8):
            total = total + blocks_ref[sender, target]
        out_ref[...] = total


def precond_kernel(me_ref, eig_ref, *refs):
    parts, blocks, out_ref, rot_in_ref = refs[:4], refs[4:8], refs[8], refs[9]
    y, _, _, x = place(me_ref)
    for k in range(4):
        source = lax.rem(x + 4 - k, 4)
        rot_in_ref[pl.ds(pl.multiple_of(source * 64, 64), 64), :] = blocks[k][:, 64:, :].reshape(64, 128)
    rot = parts[0][...] + parts[1][...] + parts[2][...] + parts[3][...]
    rot = rot.reshape(32, rot.shape[-1])
    lane_query = lax.broadcasted_iota(jnp.int32, rot.shape, 1) // QLEN
    count = rot.shape[1] // QLEN
    masked = jnp.concatenate([jnp.where(lane_query == q, rot, 0.0) for q in range(count)], 0)
    both = lax.dot_general(
        masked,
        rot_in_ref[...],
        (((1,), (0,)), ((), ())),
        precision=lax.Precision.HIGHEST,
        preferred_element_type=jnp.float32,
    ) * (1.0 / QLEN)
    for slot in range(4):
        rows = pl.ds(pl.multiple_of(8 * lax.rem(y + slot, 4), 8), 8)
        eig = eig_ref[rows, :] + DAMPING
        for q in range(count):
            out_ref[rows, q, :] = both[32 * q + 8 * slot : 32 * q + 8 * slot + 8] / eig


def basis_product(core, slabs, high_ref, low_ref, out_ref):
    total = None
    for half, group in ((core, slabs[:4]), (1 - core, slabs[4:])):
        value = jnp.concatenate([ref[...].reshape(64, HALF) for ref in group], 0)
        high, low = split(value)
        part = dot_nt(high, high_ref[half]) + dot_nt(high, low_ref[half]) + dot_nt(low, high_ref[half])
        total = part if total is None else total + part
    for slot in range(4):
        out_ref[:, 8 * slot : 8 * slot + 8, :] = total[64 * slot : 64 * slot + 64].reshape(8, 8, 512)


def train_kernel(me_ref, len_ref, grads_ref, *refs):
    blocks, slabs, (out_ref, high_ref, low_ref, total_ref) = refs[:4], refs[4:12], refs[12:]
    _, core, _, x = place(me_ref)
    step = pl.program_id(0)
    cols = grads_ref.shape[1]

    @pl.when(step == 0)
    def _():
        total_ref[...] = jnp.zeros_like(total_ref)

    for k in range(4):

        @pl.when(step == k)
        def _(k=k):
            first = lax.rem(x + 4 - k, 4) * 512
            high, low = split(blocks[k][:, :64, :].reshape(512, 128).T)
            pair = jnp.concatenate([high, low], 0)
            token = first + lax.broadcasted_iota(jnp.int32, pair.shape, 1)
            begin = jnp.int32(0)
            for doc in range(4):
                end = begin + len_ref[doc]

                @pl.when((begin < first + 512) & (end > first))
                def _(begin=begin, end=end, doc=doc):
                    masked = jnp.where((token >= begin) & (token < end), pair, jnp.zeros_like(pair))
                    both = dot_nn(masked, grads_ref[...])
                    total_ref[doc] += both[:128] + both[128:]

                begin = end

    @pl.when(step == 3)
    def _():
        for doc in range(4):
            length = jnp.full((128, cols), len_ref[doc], jnp.int32).astype(jnp.float32)
            high, low = split(total_ref[doc] / length)
            rows = slice(128 * doc, 128 * doc + 128)
            for ref, value in ((high_ref, high), (low_ref, low)):
                ref[0, rows, :] = value[:, :HALF]
                ref[1, rows, : 2 * HALF - cols] = jnp.zeros((128, 2 * HALF - cols), jnp.bfloat16)
                ref[1, rows, 2 * HALF - cols :] = value[:, HALF:]

    @pl.when(step == 4)
    def _():
        basis_product(core, slabs, high_ref, low_ref, out_ref)


def product_kernel(me_ref, high_ref, low_ref, *refs):
    slabs, out_refs = refs[:8], refs[8:]
    _, core, _, _ = place(me_ref)
    for at, out_ref in enumerate(out_refs):

        @pl.when(pl.program_id(0) == at)
        def _(out_ref=out_ref):
            basis_product(core, slabs, high_ref, low_ref, out_ref)


def score_kernel(me_ref, blocks_ref, *refs):
    preconds, out_ref = refs[:8], refs[8]
    y, core, _, _ = place(me_ref)
    train = blocks_ref[0]
    for sender in range(1, 8):
        train = train + blocks_ref[sender]
    for index, ref in enumerate(preconds):
        other, k = divmod(index, 4)
        owner = 2 * lax.rem(y + 4 - k, 4) + lax.rem(core + other, 2)
        sums = [None] * 4
        for slot in range(4):
            base = 8 * lax.rem(y + slot, 4)
            for r in range(8):
                value = ref[base + r]
                row = train[8 * slot + r : 8 * slot + r + 1]
                for doc in range(4):
                    product = value * row[:, 128 * doc : 128 * doc + 128]
                    sums[doc] = product if sums[doc] is None else sums[doc] + product
        for q in range(8):
            for doc in range(4):
                out_ref[4 * owner + q // 2, 4 * (q % 2) + doc : 4 * (q % 2) + doc + 1, :] = sums[doc][q : q + 1]


def local(
    out_grads,
    in_acts,
    query_grads,
    query_acts,
    output_basis,
    input_basis,
    eigenvalues,
    doc_ids,
    doc_lengths,
):
    f32, bf16 = jnp.float32, jnp.bfloat16
    me = lax.axis_index(("y", "core", "z", "x")).astype(jnp.int32).reshape(1)
    queries = query_grads.shape[0]

    parts = call(
        input_rotation_kernel,
        [((8, 72, 128), f32)] * 4,
        [VMEM, VMEM, pl.BlockSpec((128, in_acts.shape[1]), lambda i, me: (0, me[0] % 32))],
        me, args=(in_acts, query_acts, input_basis),
    )
    arrived = [parts[0]]
    for k in (2, 1, 3):
        arrived.append(shifted(parts[k], "x", k))
    part = arrived[0] + arrived[1] + arrived[2] + arrived[3]
    part = exchange(part, "z")
    (part,) = call(block_sum_kernel, [((8, 72, 128), f32)], [VMEM], me, args=(part,))
    block = exchange(part, "z")
    blocks = [block] + [None] * 3
    for k in (2, 1, 3):
        blocks[k] = shifted(block, "x", k)

    (picked,) = call(
        basis_pick_kernel,
        [((32, 8, HALF), f32)],
        [pl.BlockSpec((8, output_basis.shape[1]), lambda i, me: (me[0] // 64, 0))],
        me, args=(output_basis,),
    )
    slab = exchange(picked, ZX).reshape(8, 4, 8, HALF)
    slabs = [slab]
    for k in (1, 2, 3):
        slabs.append(shifted(slab, "y", 4 - k))
    for k in range(4):
        slabs.append(shifted(slabs[k], "core", 1))

    query_call = functools.partial(
        call, outs=[((8, 4, 4, 8, queries), f32)], me=me, scratch=[pltpu.VMEM((queries, HALF), bf16)]
    )
    (rot,) = query_call(functools.partial(query_kernel, True), in_specs=[VMEM] * 5, args=(query_grads, *slabs[:4]))
    (rot,) = query_call(
        functools.partial(query_kernel, False), in_specs=[VMEM] * 6, args=(query_grads, rot, *slabs[4:])
    )
    rot = exchange(rot, "z")
    rots = call(query_sum_kernel, [((4, 8, queries), f32)] * 4, [VMEM], me, args=(rot,))
    rots = [rots[0]] + [shifted(rots[k], "x", k) for k in (1, 2, 3)]
    (precond,) = call(
        precond_kernel,
        [((32, 8, 128), f32)],
        [VMEM] * 9,
        me, args=(eigenvalues, *rots, *blocks),
        scratch=[pltpu.VMEM((queries, 128), f32)],
    )
    preconds = [precond]
    for k in (1, 2, 3):
        preconds.append(shifted(precond, "y", k))
    preconds = preconds + [shifted(p, "core", 1) for p in preconds]

    def slab_specs(first, stride=0):
        return [
            pl.BlockSpec((8, 1, 8, HALF), lambda i, me: (0, lax.rem(me[0] % 4 + first + stride * i, 4), 0, 0))
        ] * 8

    block_shape, sum_shape = ((8, 32, 512), f32), ((2, 512, HALF), bf16)
    sent = [None] * 4
    sent[2], high, low = call(
        train_kernel,
        [block_shape, sum_shape, sum_shape],
        [
            SMEM,
            pl.BlockSpec((512, out_grads.shape[1]), lambda i, me: (lax.rem(me[0] % 4 + 4 - jnp.minimum(i, 3), 4), 0)),
            *[VMEM] * 4,
            *slab_specs(2),
        ],
        me,
        args=(doc_lengths, out_grads, *blocks, *slabs),
        grid=5,
        scratch=[pltpu.VMEM((4, 128, out_grads.shape[1]), f32)],
    )
    sent[1], sent[3] = call(
        product_kernel, [block_shape] * 2, [VMEM, VMEM, *slab_specs(1, 2)], me, args=(high, low, *slabs), grid=2
    )
    sent[2] = shifted(sent[2], "x", 2)
    (sent[0],) = call(
        product_kernel, [block_shape], [VMEM, VMEM, *slab_specs(0)], me, args=(high, low, *slabs)
    )
    for k in (1, 3):
        sent[k] = shifted(sent[k], "x", k)
    train = sent[0] + sent[1] + sent[2] + sent[3]
    train = exchange(train, "z")

    (partial_scores,) = call(score_kernel, [((32, 8, 128), f32)], [VMEM] * 9, me, args=(train, *preconds))
    return jnp.sum(exchange(partial_scores, ZX), axis=(0, 2)).reshape(2, 4)


def solution(mesh):
    fine = Mesh(mesh.devices.reshape(4, 2, 8, 4), ("y", "core", "z", "x"))
    seq, factor = ("y", "core"), ("z", "x")
    in_specs = (
        P(seq, factor),
        P(seq, factor),
        P(seq, factor),
        P(seq, factor),
        P(factor, None),
        P(),
        P(factor, None),
        P(seq),
        P(seq),
    )

    return jax.shard_map(local, mesh=fine, in_specs=in_specs, out_specs=P(factor, seq), check_vma=False)
```

```python
import functools

import jax
import jax.numpy as jnp
from jax import lax
from jax.experimental import pallas as pl
from jax.experimental.pallas import tpu as pltpu
from jax.sharding import Mesh, PartitionSpec as P


QLEN = 32
DAMPING = 1.0
ZX = ("z", "x")

HALF = 512
VMEM = pl.BlockSpec(memory_space=pltpu.VMEM)
SMEM = pl.BlockSpec(memory_space=pltpu.SMEM)


def exchange(blocks, axis):
    return lax.all_to_all(blocks, axis, 0, 0, tiled=True)


def shifted(shard, axis, hops):
    n = lax.axis_size(axis)
    return lax.ppermute(shard, axis, [(i, (i + hops) % n) for i in range(n)])


def call(kernel, outs, in_specs, me, *, args, grid=1, scratch=()):
    out_shape = [jax.ShapeDtypeStruct(*o) for o in outs]
    return pl.pallas_call(
        kernel,
        out_shape=out_shape,
        grid_spec=pltpu.PrefetchScalarGridSpec(
            num_scalar_prefetch=1,
            grid=(grid,),
            in_specs=in_specs,
            out_specs=[VMEM] * len(out_shape),
            scratch_shapes=list(scratch),
        ),
    )(me, *args)


def place(me_ref):
    me = me_ref[0]
    return me // 64, (me // 32) % 2, (me // 4) % 8, me % 4


def split(value):
    high = value.astype(jnp.bfloat16)
    return high, (value - high.astype(jnp.float32)).astype(jnp.bfloat16)


def dot_nt(left, right):
    return lax.dot_general(
        left, right, (((1,), (1,)), ((), ())), preferred_element_type=jnp.float32
    )


def dot_nn(left, right):
    return lax.dot_general(
        left, right, (((1,), (0,)), ((), ())), preferred_element_type=jnp.float32
    )


def input_rotation_kernel(me_ref, acts_ref, query_ref, basis_ref, *out_refs):
    _, _, _, x = place(me_ref)
    high, low = split(basis_ref[...])
    for k, out_ref in enumerate(out_refs):
        target = lax.rem(x + k, 4)
        acts = acts_ref[pl.ds(pl.multiple_of(target * 512, 512), 512), :]
        query = query_ref[pl.ds(pl.multiple_of(target * 64, 64), 64), :]
        out_ref[:, :64, :] = (dot_nt(acts, high) + dot_nt(acts, low)).reshape(8, 64, 128)
        out_ref[:, 64:, :] = (dot_nt(query, high) + dot_nt(query, low)).reshape(8, 8, 128)


def basis_pick_kernel(me_ref, basis_ref, out_ref):
    _, core, _, _ = place(me_ref)
    cols = basis_ref.shape[1] // 32
    for f in range(32):
        start = pl.multiple_of(f * cols + core * (cols - HALF), 128)
        out_ref[f] = basis_ref[:, pl.ds(start, HALF)]


def query_kernel(own, me_ref, grads_ref, *refs):
    so_far = None if own else refs[0]
    slabs, out_ref, half_ref = refs[-6:-2], refs[-2], refs[-1]
    _, core, _, _ = place(me_ref)
    cols = grads_ref.shape[1]
    half = core if own else 1 - core

    @pl.when(half == 0)
    def _():
        half_ref[...] = grads_ref[:, :HALF]

    @pl.when(half == 1)
    def _():
        half_ref[:, : 2 * HALF - cols] = jnp.zeros((grads_ref.shape[0], 2 * HALF - cols), jnp.bfloat16)
        half_ref[:, 2 * HALF - cols :] = grads_ref[:, HALF:]

    for slot in range(4):
        high, low = split(slabs[slot][...].reshape(256, HALF))
        total = (dot_nt(high, half_ref[...]) + dot_nt(low, half_ref[...])).reshape(8, 4, 8, half_ref.shape[0])
        out_ref[:, :, slot] = total if own else so_far[:, :, slot] + total


def query_sum_kernel(me_ref, blocks_ref, *out_refs):
    _, _, _, x = place(me_ref)
    for k, out_ref in enumerate(out_refs):
        target = lax.rem(x + k, 4)
        total = blocks_ref[0, target]
        for sender in range(1, 8):
            total = total + blocks_ref[sender, target]
        out_ref[...] = total


def precond_kernel(me_ref, eig_ref, *refs):
    parts, blocks, out_ref, rot_in_ref = refs[:4], refs[4:8], refs[8], refs[9]
    y, _, _, x = place(me_ref)
    for k in range(4):
        source = lax.rem(x + 4 - k, 4)
        rot_in_ref[pl.ds(pl.multiple_of(source * 64, 64), 64), :] = blocks[k][:, 64:, :].reshape(64, 128)
    rot = parts[0][...] + parts[1][...] + parts[2][...] + parts[3][...]
    rot = rot.reshape(32, rot.shape[-1])
    lane_query = lax.broadcasted_iota(jnp.int32, rot.shape, 1) // QLEN
    count = rot.shape[1] // QLEN
    masked = jnp.concatenate([jnp.where(lane_query == q, rot, 0.0) for q in range(count)], 0)
    both = lax.dot_general(
        masked,
        rot_in_ref[...],
        (((1,), (0,)), ((), ())),
        precision=lax.Precision.HIGHEST,
        preferred_element_type=jnp.float32,
    ) * (1.0 / QLEN)
    for slot in range(4):
        rows = pl.ds(pl.multiple_of(8 * lax.rem(y + slot, 4), 8), 8)
        eig = eig_ref[rows, :] + DAMPING
        for q in range(count):
            out_ref[rows, q, :] = both[32 * q + 8 * slot : 32 * q + 8 * slot + 8] / eig


def basis_product(core, slabs, high_ref, low_ref, out_ref):
    total = None
    for half, group in ((core, slabs[:4]), (1 - core, slabs[4:])):
        value = jnp.concatenate([ref[...].reshape(64, HALF) for ref in group], 0)
        high, low = split(value)
        part = dot_nt(high, high_ref[half]) + dot_nt(high, low_ref[half]) + dot_nt(low, high_ref[half])
        total = part if total is None else total + part
    for slot in range(4):
        out_ref[:, 8 * slot : 8 * slot + 8, :] = total[64 * slot : 64 * slot + 64].reshape(8, 8, 512)


def train_kernel(me_ref, len_ref, grads_ref, *refs):
    blocks, slabs, (out_ref, high_ref, low_ref, total_ref) = refs[:4], refs[4:12], refs[12:]
    _, core, _, x = place(me_ref)
    step = pl.program_id(0)
    cols = grads_ref.shape[1]

    @pl.when(step == 0)
    def _():
        total_ref[...] = jnp.zeros_like(total_ref)

    for k in range(4):

        @pl.when(step == k)
        def _(k=k):
            first = lax.rem(x + 4 - k, 4) * 512
            high, low = split(blocks[k][:, :64, :].reshape(512, 128).T)
            pair = jnp.concatenate([high, low], 0)
            token = first + lax.broadcasted_iota(jnp.int32, pair.shape, 1)
            begin = jnp.int32(0)
            for doc in range(4):
                end = begin + len_ref[doc]

                @pl.when((begin < first + 512) & (end > first))
                def _(begin=begin, end=end, doc=doc):
                    masked = jnp.where((token >= begin) & (token < end), pair, jnp.zeros_like(pair))
                    both = dot_nn(masked, grads_ref[...])
                    total_ref[doc] += both[:128] + both[128:]

                begin = end

    @pl.when(step == 3)
    def _():
        for doc in range(4):
            length = jnp.full((128, cols), len_ref[doc], jnp.int32).astype(jnp.float32)
            high, low = split(total_ref[doc] / length)
            rows = slice(128 * doc, 128 * doc + 128)
            for ref, value in ((high_ref, high), (low_ref, low)):
                ref[0, rows, :] = value[:, :HALF]
                ref[1, rows, : 2 * HALF - cols] = jnp.zeros((128, 2 * HALF - cols), jnp.bfloat16)
                ref[1, rows, 2 * HALF - cols :] = value[:, HALF:]

    @pl.when(step == 4)
    def _():
        basis_product(core, slabs, high_ref, low_ref, out_ref)


def product_kernel(me_ref, high_ref, low_ref, *refs):
    slabs, out_refs = refs[:8], refs[8:]
    _, core, _, _ = place(me_ref)
    for at, out_ref in enumerate(out_refs):

        @pl.when(pl.program_id(0) == at)
        def _(out_ref=out_ref):
            basis_product(core, slabs, high_ref, low_ref, out_ref)


def score_kernel(me_ref, blocks_ref, *refs):
    preconds, out_ref = refs[:8], refs[8]
    y, core, _, _ = place(me_ref)
    train = blocks_ref[0]
    for sender in range(1, 8):
        train = train + blocks_ref[sender]
    for index, ref in enumerate(preconds):
        other, k = divmod(index, 4)
        owner = 2 * lax.rem(y + 4 - k, 4) + lax.rem(core + other, 2)
        sums = [None] * 4
        for slot in range(4):
            base = 8 * lax.rem(y + slot, 4)
            for r in range(8):
                value = ref[base + r]
                row = train[8 * slot + r : 8 * slot + r + 1]
                for doc in range(4):
                    product = value * row[:, 128 * doc : 128 * doc + 128]
                    sums[doc] = product if sums[doc] is None else sums[doc] + product
        for q in range(8):
            for doc in range(4):
                out_ref[4 * owner + q // 2, 4 * (q % 2) + doc : 4 * (q % 2) + doc + 1, :] = sums[doc][q : q + 1]


def local(
    out_grads,
    in_acts,
    query_grads,
    query_acts,
    output_basis,
    input_basis,
    eigenvalues,
    doc_ids,
    doc_lengths,
):
    f32, bf16 = jnp.float32, jnp.bfloat16
    me = lax.axis_index(("y", "core", "z", "x")).astype(jnp.int32).reshape(1)
    queries = query_grads.shape[0]

    parts = call(
        input_rotation_kernel,
        [((8, 72, 128), f32)] * 4,
        [VMEM, VMEM, pl.BlockSpec((128, in_acts.shape[1]), lambda i, me: (0, me[0] % 32))],
        me, args=(in_acts, query_acts, input_basis),
    )
    arrived = [parts[0]]
    for k in (2, 1, 3):
        arrived.append(shifted(parts[k], "x", k))
    part = arrived[0] + arrived[1] + arrived[2] + arrived[3]
    part = exchange(part, "z")
    part = jnp.broadcast_to(jnp.sum(part, axis=0)[None], (8, 72, 128))
    block = exchange(part, "z")
    blocks = [block] + [None] * 3
    for k in (2, 1, 3):
        blocks[k] = shifted(block, "x", k)

    (picked,) = call(
        basis_pick_kernel,
        [((32, 8, HALF), f32)],
        [pl.BlockSpec((8, output_basis.shape[1]), lambda i, me: (me[0] // 64, 0))],
        me, args=(output_basis,),
    )
    slab = exchange(picked, ZX).reshape(8, 4, 8, HALF)
    slabs = [slab]
    for k in (1, 2, 3):
        slabs.append(shifted(slab, "y", 4 - k))
    for k in range(4):
        slabs.append(shifted(slabs[k], "core", 1))

    query_call = functools.partial(
        call, outs=[((8, 4, 4, 8, queries), f32)], me=me, scratch=[pltpu.VMEM((queries, HALF), bf16)]
    )
    (rot,) = query_call(functools.partial(query_kernel, True), in_specs=[VMEM] * 5, args=(query_grads, *slabs[:4]))
    (rot,) = query_call(
        functools.partial(query_kernel, False), in_specs=[VMEM] * 6, args=(query_grads, rot, *slabs[4:])
    )
    rot = exchange(rot, "z")
    rots = call(query_sum_kernel, [((4, 8, queries), f32)] * 4, [VMEM], me, args=(rot,))
    rots = [rots[0]] + [shifted(rots[k], "x", k) for k in (1, 2, 3)]
    (precond,) = call(
        precond_kernel,
        [((32, 8, 128), f32)],
        [VMEM] * 9,
        me, args=(eigenvalues, *rots, *blocks),
        scratch=[pltpu.VMEM((queries, 128), f32)],
    )
    preconds = [precond]
    for k in (1, 2, 3):
        preconds.append(shifted(precond, "y", k))
    preconds = preconds + [shifted(p, "core", 1) for p in preconds]

    def slab_specs(first, stride=0):
        return [
            pl.BlockSpec((8, 1, 8, HALF), lambda i, me: (0, lax.rem(me[0] % 4 + first + stride * i, 4), 0, 0))
        ] * 8

    block_shape, sum_shape = ((8, 32, 512), f32), ((2, 512, HALF), bf16)
    sent = [None] * 4
    sent[2], high, low = call(
        train_kernel,
        [block_shape, sum_shape, sum_shape],
        [
            SMEM,
            pl.BlockSpec((512, out_grads.shape[1]), lambda i, me: (lax.rem(me[0] % 4 + 4 - jnp.minimum(i, 3), 4), 0)),
            *[VMEM] * 4,
            *slab_specs(2),
        ],
        me,
        args=(doc_lengths, out_grads, *blocks, *slabs),
        grid=5,
        scratch=[pltpu.VMEM((4, 128, out_grads.shape[1]), f32)],
    )
    sent[1], sent[3] = call(
        product_kernel, [block_shape] * 2, [VMEM, VMEM, *slab_specs(1, 2)], me, args=(high, low, *slabs), grid=2
    )
    sent[2] = shifted(sent[2], "x", 2)
    (sent[0],) = call(
        product_kernel, [block_shape], [VMEM, VMEM, *slab_specs(0)], me, args=(high, low, *slabs)
    )
    for k in (1, 3):
        sent[k] = shifted(sent[k], "x", k)
    train = sent[0] + sent[1] + sent[2] + sent[3]
    train = exchange(train, "z")

    (partial_scores,) = call(score_kernel, [((32, 8, 128), f32)], [VMEM] * 9, me, args=(train, *preconds))
    return jnp.sum(exchange(partial_scores, ZX), axis=(0, 2)).reshape(2, 4)


def solution(mesh):
    fine = Mesh(mesh.devices.reshape(4, 2, 8, 4), ("y", "core", "z", "x"))
    seq, factor = ("y", "core"), ("z", "x")
    in_specs = (
        P(seq, factor),
        P(seq, factor),
        P(seq, factor),
        P(seq, factor),
        P(factor, None),
        P(),
        P(factor, None),
        P(seq),
        P(seq),
    )

    return jax.shard_map(local, mesh=fine, in_specs=in_specs, out_specs=P(factor, seq), check_vma=False)
```

```python
import functools

import jax
import jax.numpy as jnp
from jax import lax
from jax.experimental import pallas as pl
from jax.experimental.pallas import tpu as pltpu
from jax.sharding import Mesh, PartitionSpec as P


QLEN = 32
DAMPING = 1.0
ZX = ("z", "x")

HALF = 512
VMEM = pl.BlockSpec(memory_space=pltpu.VMEM)
HELD = pl.BlockSpec(memory_space=pltpu.VMEM)
SMEM = pl.BlockSpec(memory_space=pltpu.SMEM)


def exchange(blocks, axis):
    return lax.all_to_all(blocks, axis, 0, 0, tiled=True)


def shifted(shard, axis, hops):
    n = lax.axis_size(axis)
    return lax.ppermute(shard, axis, [(i, (i + hops) % n) for i in range(n)])


def call(kernel, outs, in_specs, me, *, args, grid=1, scratch=(), held=True):
    out_shape = [(pltpu.VMEM if held else pltpu.HBM)(*o) for o in outs]
    spaces = [pltpu.VMEM if spec is HELD else None if spec.block_shape is None else pltpu.HBM for spec in in_specs]
    args = [a if space is None else pltpu.with_memory_space_constraint(a, space) for a, space in zip(args, spaces)]
    return pl.pallas_call(
        kernel,
        out_shape=out_shape,
        grid_spec=pltpu.PrefetchScalarGridSpec(
            num_scalar_prefetch=1,
            grid=(grid,),
            in_specs=in_specs,
            out_specs=[VMEM] * len(out_shape),
            scratch_shapes=list(scratch),
        ),
        compiler_params=pltpu.CompilerParams(vmem_limit_bytes=28 << 20),
    )(me, *args)


def place(me_ref):
    me = me_ref[0]
    return me // 64, (me // 32) % 2, (me // 4) % 8, me % 4


def split(value):
    high = value.astype(jnp.bfloat16)
    return high, (value - high.astype(jnp.float32)).astype(jnp.bfloat16)


def dot_nt(left, right):
    return lax.dot_general(
        left, right, (((1,), (1,)), ((), ())), preferred_element_type=jnp.float32
    )


def dot_nn(left, right):
    return lax.dot_general(
        left, right, (((1,), (0,)), ((), ())), preferred_element_type=jnp.float32
    )


def input_rotation_kernel(me_ref, acts_ref, query_ref, basis_ref, *out_refs):
    _, _, _, x = place(me_ref)
    high, low = split(basis_ref[...])
    for k, out_ref in enumerate(out_refs):
        target = lax.rem(x + k, 4)
        acts = acts_ref[pl.ds(pl.multiple_of(target * 512, 512), 512), :]
        query = query_ref[pl.ds(pl.multiple_of(target * 64, 64), 64), :]
        out_ref[:, :64, :] = (dot_nt(acts, high) + dot_nt(acts, low)).reshape(8, 64, 128)
        out_ref[:, 64:, :] = (dot_nt(query, high) + dot_nt(query, low)).reshape(8, 8, 128)


def basis_pick_kernel(me_ref, basis_ref, out_ref):
    _, core, _, _ = place(me_ref)
    cols = basis_ref.shape[1] // 32
    for f in range(32):
        start = pl.multiple_of(f * cols + core * (cols - HALF), 128)
        out_ref[f] = basis_ref[:, pl.ds(start, HALF)]


def query_kernel(own, me_ref, grads_ref, *refs):
    so_far = None if own else refs[0]
    slabs, out_ref, half_ref = refs[-6:-2], refs[-2], refs[-1]
    _, core, _, _ = place(me_ref)
    cols = grads_ref.shape[1]
    half = core if own else 1 - core

    @pl.when(half == 0)
    def _():
        half_ref[...] = grads_ref[:, :HALF]

    @pl.when(half == 1)
    def _():
        half_ref[:, : 2 * HALF - cols] = jnp.zeros((grads_ref.shape[0], 2 * HALF - cols), jnp.bfloat16)
        half_ref[:, 2 * HALF - cols :] = grads_ref[:, HALF:]

    for slot in range(4):
        high, low = split(slabs[slot][...].reshape(256, HALF))
        total = (dot_nt(high, half_ref[...]) + dot_nt(low, half_ref[...])).reshape(8, 4, 8, half_ref.shape[0])
        out_ref[:, :, slot] = total if own else so_far[:, :, slot] + total


def query_sum_kernel(me_ref, blocks_ref, *out_refs):
    _, _, _, x = place(me_ref)
    for k, out_ref in enumerate(out_refs):
        target = lax.rem(x + k, 4)
        total = blocks_ref[0, target]
        for sender in range(1, 8):
            total = total + blocks_ref[sender, target]
        out_ref[...] = total


def precond_kernel(me_ref, eig_ref, *refs):
    parts, blocks, out_ref, rot_in_ref = refs[:4], refs[4:8], refs[8], refs[9]
    y, _, _, x = place(me_ref)
    for k in range(4):
        source = lax.rem(x + 4 - k, 4)
        rot_in_ref[pl.ds(pl.multiple_of(source * 64, 64), 64), :] = blocks[k][:, 64:, :].reshape(64, 128)
    rot = parts[0][...] + parts[1][...] + parts[2][...] + parts[3][...]
    rot = rot.reshape(32, rot.shape[-1])
    lane_query = lax.broadcasted_iota(jnp.int32, rot.shape, 1) // QLEN
    count = rot.shape[1] // QLEN
    masked = jnp.concatenate([jnp.where(lane_query == q, rot, 0.0) for q in range(count)], 0)
    both = lax.dot_general(
        masked,
        rot_in_ref[...],
        (((1,), (0,)), ((), ())),
        precision=lax.Precision.HIGHEST,
        preferred_element_type=jnp.float32,
    ) * (1.0 / QLEN)
    for slot in range(4):
        rows = pl.ds(pl.multiple_of(8 * lax.rem(y + slot, 4), 8), 8)
        eig = eig_ref[rows, :] + DAMPING
        for q in range(count):
            out_ref[rows, q, :] = both[32 * q + 8 * slot : 32 * q + 8 * slot + 8] / eig


def basis_product(me_ref, hops, slabs, high_ref, low_ref, out_ref):
    _, core, _, x = place(me_ref)
    target = lax.rem(x + hops, 4)
    total = None
    for half, group in ((core, slabs[:4]), (1 - core, slabs[4:])):
        value = jnp.concatenate([ref[:, target].reshape(64, HALF) for ref in group], 0)
        high, low = split(value)
        part = dot_nt(high, high_ref[half]) + dot_nt(high, low_ref[half]) + dot_nt(low, high_ref[half])
        total = part if total is None else total + part
    for slot in range(4):
        out_ref[:, 8 * slot : 8 * slot + 8, :] = total[64 * slot : 64 * slot + 64].reshape(8, 8, 512)


def train_kernel(me_ref, len_ref, grads_ref, *refs):
    blocks, slabs, (out_ref, high_ref, low_ref, total_ref) = refs[:4], refs[4:12], refs[12:]
    _, _, _, x = place(me_ref)
    step = pl.program_id(0)
    cols = grads_ref.shape[1]

    @pl.when(step == 0)
    def _():
        total_ref[...] = jnp.zeros_like(total_ref)

    for k in range(4):

        @pl.when(step == k)
        def _(k=k):
            first = lax.rem(x + 4 - k, 4) * 512
            high, low = split(blocks[k][:, :64, :].reshape(512, 128).T)
            pair = jnp.concatenate([high, low], 0)
            token = first + lax.broadcasted_iota(jnp.int32, pair.shape, 1)
            begin = jnp.int32(0)
            for doc in range(4):
                end = begin + len_ref[doc]

                @pl.when((begin < first + 512) & (end > first))
                def _(begin=begin, end=end, doc=doc):
                    masked = jnp.where((token >= begin) & (token < end), pair, jnp.zeros_like(pair))
                    both = dot_nn(masked, grads_ref[...])
                    total_ref[doc] += both[:128] + both[128:]

                begin = end

    @pl.when(step == 3)
    def _():
        for doc in range(4):
            length = jnp.full((128, cols), len_ref[doc], jnp.int32).astype(jnp.float32)
            high, low = split(total_ref[doc] / length)
            rows = slice(128 * doc, 128 * doc + 128)
            for ref, value in ((high_ref, high), (low_ref, low)):
                ref[0, rows, :] = value[:, :HALF]
                ref[1, rows, : 2 * HALF - cols] = jnp.zeros((128, 2 * HALF - cols), jnp.bfloat16)
                ref[1, rows, 2 * HALF - cols :] = value[:, HALF:]

    @pl.when(step == 4)
    def _():
        basis_product(me_ref, 2, slabs, high_ref, low_ref, out_ref)


def product_kernel(hops, me_ref, high_ref, low_ref, *refs):
    slabs, out_refs = refs[:8], refs[8:]
    for k, out_ref in zip(hops, out_refs):
        basis_product(me_ref, k, slabs, high_ref, low_ref, out_ref)


def score_kernel(me_ref, blocks_ref, *refs):
    preconds, out_ref = refs[:8], refs[8]
    y, core, _, _ = place(me_ref)
    train = blocks_ref[0]
    for sender in range(1, 8):
        train = train + blocks_ref[sender]
    for index, ref in enumerate(preconds):
        other, k = divmod(index, 4)
        owner = 2 * lax.rem(y + 4 - k, 4) + lax.rem(core + other, 2)
        sums = [None] * 4
        for slot in range(4):
            base = 8 * lax.rem(y + slot, 4)
            for r in range(8):
                value = ref[base + r]
                row = train[8 * slot + r : 8 * slot + r + 1]
                for doc in range(4):
                    product = value * row[:, 128 * doc : 128 * doc + 128]
                    sums[doc] = product if sums[doc] is None else sums[doc] + product
        for q in range(8):
            for doc in range(4):
                out_ref[4 * owner + q // 2, 4 * (q % 2) + doc : 4 * (q % 2) + doc + 1, :] = sums[doc][q : q + 1]


def local(
    out_grads,
    in_acts,
    query_grads,
    query_acts,
    output_basis,
    input_basis,
    eigenvalues,
    doc_ids,
    doc_lengths,
):
    f32, bf16 = jnp.float32, jnp.bfloat16
    me = lax.axis_index(("y", "core", "z", "x")).astype(jnp.int32).reshape(1)
    queries = query_grads.shape[0]

    parts = call(
        input_rotation_kernel,
        [((8, 72, 128), f32)] * 4,
        [VMEM, VMEM, pl.BlockSpec((128, in_acts.shape[1]), lambda i, me: (0, me[0] % 32))],
        me, args=(in_acts, query_acts, input_basis),
    )
    arrived = [parts[0]]
    for k in (2, 1, 3):
        arrived.append(shifted(parts[k], "x", k))
    part = arrived[0] + arrived[1] + arrived[2] + arrived[3]
    part = exchange(part, "z")
    part = jnp.broadcast_to(jnp.sum(part, axis=0)[None], (8, 72, 128))
    block = exchange(part, "z")
    blocks = [block] + [None] * 3
    for k in (2, 1, 3):
        blocks[k] = shifted(block, "x", k)

    (picked,) = call(
        basis_pick_kernel,
        [((32, 8, HALF), f32)],
        [pl.BlockSpec((8, output_basis.shape[1]), lambda i, me: (me[0] // 64, 0))],
        me, args=(output_basis,), held=False,
    )
    slab = exchange(picked, ZX).reshape(8, 4, 8, HALF)
    slabs = [slab]
    for k in (1, 2, 3):
        slabs.append(shifted(slab, "y", 4 - k))
    for k in range(4):
        slabs.append(shifted(slabs[k], "core", 1))

    query_call = functools.partial(
        call, outs=[((8, 4, 4, 8, queries), f32)], me=me, scratch=[pltpu.VMEM((queries, HALF), bf16)]
    )
    (rot,) = query_call(functools.partial(query_kernel, True), in_specs=[VMEM] + [HELD] * 4, args=(query_grads, *slabs[:4]))
    (rot,) = query_call(
        functools.partial(query_kernel, False),
        in_specs=[VMEM] + [HELD] * 5,
        args=(query_grads, rot, *slabs[4:]),
        held=False,
    )
    rot = exchange(rot, "z")
    rots = call(query_sum_kernel, [((4, 8, queries), f32)] * 4, [HELD], me, args=(rot,))
    rots = [rots[0]] + [shifted(rots[k], "x", k) for k in (1, 2, 3)]
    (precond,) = call(
        precond_kernel,
        [((32, 8, 128), f32)],
        [VMEM] + [HELD] * 8,
        me, args=(eigenvalues, *rots, *blocks),
        scratch=[pltpu.VMEM((queries, 128), f32)],
    )
    preconds = [precond]
    for k in (1, 2, 3):
        preconds.append(shifted(precond, "y", k))
    preconds = preconds + [shifted(p, "core", 1) for p in preconds]

    block_shape, sum_shape = ((8, 32, 512), f32), ((2, 512, HALF), bf16)
    sent = [None] * 4
    sent[2], high, low = call(
        train_kernel,
        [block_shape, sum_shape, sum_shape],
        [
            SMEM,
            pl.BlockSpec((512, out_grads.shape[1]), lambda i, me: (lax.rem(me[0] % 4 + 4 - jnp.minimum(i, 3), 4), 0)),
            *[HELD] * 12,
        ],
        me,
        args=(doc_lengths, out_grads, *blocks, *slabs),
        grid=5,
        scratch=[pltpu.VMEM((4, 128, out_grads.shape[1]), f32)],
    )
    sent[1], sent[3] = call(
        functools.partial(product_kernel, (1, 3)), [block_shape] * 2, [HELD] * 10, me, args=(high, low, *slabs)
    )
    sent[2] = shifted(sent[2], "x", 2)
    (sent[0],) = call(
        functools.partial(product_kernel, (0,)), [block_shape], [HELD] * 10, me, args=(high, low, *slabs), held=False
    )
    for k in (1, 3):
        sent[k] = shifted(sent[k], "x", k)
    train = sent[0] + sent[1] + sent[2] + sent[3]
    train = exchange(train, "z")

    (partial_scores,) = call(score_kernel, [((32, 8, 128), f32)], [HELD] * 9, me, args=(train, *preconds))
    return jnp.sum(exchange(partial_scores, ZX), axis=(0, 2)).reshape(2, 4)


def solution(mesh):
    fine = Mesh(mesh.devices.reshape(4, 2, 8, 4), ("y", "core", "z", "x"))
    seq, factor = ("y", "core"), ("z", "x")
    in_specs = (
        P(seq, factor),
        P(seq, factor),
        P(seq, factor),
        P(seq, factor),
        P(factor, None),
        P(),
        P(factor, None),
        P(seq),
        P(seq),
    )

    return jax.shard_map(local, mesh=fine, in_specs=in_specs, out_specs=P(factor, seq), check_vma=False)
```

```python
import functools

import jax
import jax.numpy as jnp
from jax import lax
from jax.experimental import pallas as pl
from jax.experimental.pallas import tpu as pltpu
from jax.sharding import Mesh, PartitionSpec as P


QLEN = 32
DAMPING = 1.0
ZX = ("z", "x")

HALF = 512
VMEM = pl.BlockSpec(memory_space=pltpu.VMEM)
HELD = pl.BlockSpec(memory_space=pltpu.VMEM)
SMEM = pl.BlockSpec(memory_space=pltpu.SMEM)
ANY = pl.BlockSpec(memory_space=pl.ANY)


def exchange(blocks, axis):
    return lax.all_to_all(blocks, axis, 0, 0, tiled=True)


def shifted(shard, axis, hops):
    n = lax.axis_size(axis)
    return lax.ppermute(shard, axis, [(i, (i + hops) % n) for i in range(n)])


def call(kernel, outs, in_specs, me, *, args, grid=1, scratch=(), held=True, out_spec=VMEM):
    out_shape = [(pltpu.VMEM if held else pltpu.HBM)(*o) for o in outs]
    spaces = [pltpu.VMEM if spec is HELD else None if spec is SMEM else pltpu.HBM for spec in in_specs]
    args = [a if space is None else pltpu.with_memory_space_constraint(a, space) for a, space in zip(args, spaces)]
    return pl.pallas_call(
        kernel,
        out_shape=out_shape,
        grid_spec=pltpu.PrefetchScalarGridSpec(
            num_scalar_prefetch=1,
            grid=(grid,),
            in_specs=in_specs,
            out_specs=[out_spec] * len(out_shape),
            scratch_shapes=list(scratch),
        ),
        compiler_params=pltpu.CompilerParams(vmem_limit_bytes=28 << 20),
    )(me, *args)


def place(me_ref):
    me = me_ref[0]
    return me // 64, (me // 32) % 2, (me // 4) % 8, me % 4


def split(value):
    high = value.astype(jnp.bfloat16)
    return high, (value - high.astype(jnp.float32)).astype(jnp.bfloat16)


def dot_nt(left, right):
    return lax.dot_general(
        left, right, (((1,), (1,)), ((), ())), preferred_element_type=jnp.float32
    )


def dot_nn(left, right):
    return lax.dot_general(
        left, right, (((1,), (0,)), ((), ())), preferred_element_type=jnp.float32
    )


def input_rotation_kernel(me_ref, acts_ref, query_ref, basis_ref, *out_refs):
    _, _, _, x = place(me_ref)
    high, low = split(basis_ref[...])
    for k, out_ref in enumerate(out_refs):
        target = lax.rem(x + k, 4)
        acts = acts_ref[pl.ds(pl.multiple_of(target * 512, 512), 512), :]
        query = query_ref[pl.ds(pl.multiple_of(target * 64, 64), 64), :]
        out_ref[:, :64, :] = (dot_nt(acts, high) + dot_nt(acts, low)).reshape(8, 64, 128)
        out_ref[:, 64:, :] = (dot_nt(query, high) + dot_nt(query, low)).reshape(8, 8, 128)


def basis_pick_kernel(me_ref, basis_ref, out_ref, sems):
    y, core, _, _ = place(me_ref)
    cols = basis_ref.shape[1] // 32
    rows = pl.ds(pl.multiple_of(8 * y, 8), 8)
    copies = []
    for f in range(32):
        start = pl.multiple_of(f * cols + core * (cols - HALF), 128)
        copies.append(pltpu.make_async_copy(basis_ref.at[rows, pl.ds(start, HALF)], out_ref.at[f], sems.at[f]))
        copies[-1].start()
    for copy in copies:
        copy.wait()


def query_kernel(own, me_ref, grads_ref, *refs):
    so_far = None if own else refs[0]
    slabs, out_ref, half_ref = refs[-6:-2], refs[-2], refs[-1]
    _, core, _, _ = place(me_ref)
    cols = grads_ref.shape[1]
    half = core if own else 1 - core

    @pl.when(half == 0)
    def _():
        half_ref[...] = grads_ref[:, :HALF]

    @pl.when(half == 1)
    def _():
        half_ref[:, : 2 * HALF - cols] = jnp.zeros((grads_ref.shape[0], 2 * HALF - cols), jnp.bfloat16)
        half_ref[:, 2 * HALF - cols :] = grads_ref[:, HALF:]

    for slot in range(4):
        high, low = split(slabs[slot][...].reshape(256, HALF))
        total = (dot_nt(high, half_ref[...]) + dot_nt(low, half_ref[...])).reshape(8, 4, 8, half_ref.shape[0])
        out_ref[:, :, slot] = total if own else so_far[:, :, slot] + total


def precond_kernel(me_ref, eig_ref, *refs):
    parts_ref, blocks, out_ref, rot_in_ref = refs[0], refs[1:5], refs[5], refs[6]
    y, _, _, x = place(me_ref)
    for k in range(4):
        source = lax.rem(x + 4 - k, 4)
        rot_in_ref[pl.ds(pl.multiple_of(source * 64, 64), 64), :] = blocks[k][:, 64:, :].reshape(64, 128)
    rot = parts_ref[0]
    for sender in range(1, 32):
        rot = rot + parts_ref[sender]
    rot = rot.reshape(32, rot.shape[-1])
    lane_query = lax.broadcasted_iota(jnp.int32, rot.shape, 1) // QLEN
    count = rot.shape[1] // QLEN
    masked = jnp.concatenate([jnp.where(lane_query == q, rot, 0.0) for q in range(count)], 0)
    both = lax.dot_general(
        masked,
        rot_in_ref[...],
        (((1,), (0,)), ((), ())),
        precision=lax.Precision.HIGHEST,
        preferred_element_type=jnp.float32,
    ) * (1.0 / QLEN)
    for slot in range(4):
        rows = pl.ds(pl.multiple_of(8 * lax.rem(y + slot, 4), 8), 8)
        eig = eig_ref[rows, :] + DAMPING
        for q in range(count):
            out_ref[rows, q, :] = both[32 * q + 8 * slot : 32 * q + 8 * slot + 8] / eig


def basis_product(me_ref, hops, slabs, high_ref, low_ref, out_ref):
    _, core, _, x = place(me_ref)
    target = lax.rem(x + hops, 4)
    total = None
    for half, group in ((core, slabs[:4]), (1 - core, slabs[4:])):
        value = jnp.concatenate([ref[:, target].reshape(64, HALF) for ref in group], 0)
        high, low = split(value)
        part = dot_nt(high, high_ref[half]) + dot_nt(high, low_ref[half]) + dot_nt(low, high_ref[half])
        total = part if total is None else total + part
    for slot in range(4):
        out_ref[:, 8 * slot : 8 * slot + 8, :] = total[64 * slot : 64 * slot + 64].reshape(8, 8, 512)


def train_kernel(me_ref, len_ref, grads_ref, *refs):
    blocks, slabs, (out_ref, high_ref, low_ref, total_ref) = refs[:4], refs[4:12], refs[12:]
    _, _, _, x = place(me_ref)
    step = pl.program_id(0)
    cols = grads_ref.shape[1]

    @pl.when(step == 0)
    def _():
        total_ref[...] = jnp.zeros_like(total_ref)

    for k in range(4):

        @pl.when(step == k)
        def _(k=k):
            first = lax.rem(x + 4 - k, 4) * 512
            high, low = split(blocks[k][:, :64, :].reshape(512, 128).T)
            pair = jnp.concatenate([high, low], 0)
            token = first + lax.broadcasted_iota(jnp.int32, pair.shape, 1)
            begin = jnp.int32(0)
            for doc in range(4):
                end = begin + len_ref[doc]

                @pl.when((begin < first + 512) & (end > first))
                def _(begin=begin, end=end, doc=doc):
                    masked = jnp.where((token >= begin) & (token < end), pair, jnp.zeros_like(pair))
                    both = dot_nn(masked, grads_ref[...])
                    total_ref[doc] += both[:128] + both[128:]

                begin = end

    @pl.when(step == 3)
    def _():
        for doc in range(4):
            length = jnp.full((128, cols), len_ref[doc], jnp.int32).astype(jnp.float32)
            high, low = split(total_ref[doc] / length)
            rows = slice(128 * doc, 128 * doc + 128)
            for ref, value in ((high_ref, high), (low_ref, low)):
                ref[0, rows, :] = value[:, :HALF]
                ref[1, rows, : 2 * HALF - cols] = jnp.zeros((128, 2 * HALF - cols), jnp.bfloat16)
                ref[1, rows, 2 * HALF - cols :] = value[:, HALF:]

    @pl.when(step == 4)
    def _():
        basis_product(me_ref, 2, slabs, high_ref, low_ref, out_ref)


def product_kernel(hops, me_ref, high_ref, low_ref, *refs):
    slabs, out_refs = refs[:8], refs[8:]
    for k, out_ref in zip(hops, out_refs):
        basis_product(me_ref, k, slabs, high_ref, low_ref, out_ref)


def score_kernel(me_ref, blocks_ref, *refs):
    preconds, out_ref = refs[:8], refs[8]
    y, core, _, _ = place(me_ref)
    train = blocks_ref[0]
    for sender in range(1, 8):
        train = train + blocks_ref[sender]
    for index, ref in enumerate(preconds):
        other, k = divmod(index, 4)
        owner = 2 * lax.rem(y + 4 - k, 4) + lax.rem(core + other, 2)
        sums = [None] * 4
        for slot in range(4):
            base = 8 * lax.rem(y + slot, 4)
            for r in range(8):
                value = ref[base + r]
                row = train[8 * slot + r : 8 * slot + r + 1]
                for doc in range(4):
                    product = value * row[:, 128 * doc : 128 * doc + 128]
                    sums[doc] = product if sums[doc] is None else sums[doc] + product
        for q in range(8):
            for doc in range(4):
                out_ref[4 * owner + q // 2, 4 * (q % 2) + doc : 4 * (q % 2) + doc + 1, :] = sums[doc][q : q + 1]


def local(
    out_grads,
    in_acts,
    query_grads,
    query_acts,
    output_basis,
    input_basis,
    eigenvalues,
    doc_ids,
    doc_lengths,
):
    f32, bf16 = jnp.float32, jnp.bfloat16
    me = lax.axis_index(("y", "core", "z", "x")).astype(jnp.int32).reshape(1)
    queries = query_grads.shape[0]

    parts = call(
        input_rotation_kernel,
        [((8, 72, 128), f32)] * 4,
        [VMEM, VMEM, pl.BlockSpec((128, in_acts.shape[1]), lambda i, me: (0, me[0] % 32))],
        me, args=(in_acts, query_acts, input_basis),
    )
    arrived = [parts[0]]
    for k in (2, 1, 3):
        arrived.append(shifted(parts[k], "x", k))
    part = arrived[0] + arrived[1] + arrived[2] + arrived[3]
    part = exchange(part, "z")
    part = jnp.broadcast_to(jnp.sum(part, axis=0)[None], (8, 72, 128))
    block = exchange(part, "z")
    blocks = [block] + [None] * 3
    for k in (2, 1, 3):
        blocks[k] = shifted(block, "x", k)

    (picked,) = call(
        basis_pick_kernel,
        [((32, 8, HALF), f32)],
        [ANY],
        me, args=(output_basis,), held=False, out_spec=ANY,
        scratch=[pltpu.SemaphoreType.DMA((32,))],
    )
    slab = exchange(picked, ZX).reshape(8, 4, 8, HALF)
    slabs = [slab]
    for k in (1, 2, 3):
        slabs.append(shifted(slab, "y", 4 - k))
    for k in range(4):
        slabs.append(shifted(slabs[k], "core", 1))

    query_call = functools.partial(
        call, outs=[((8, 4, 4, 8, queries), f32)], me=me, scratch=[pltpu.VMEM((queries, HALF), bf16)]
    )
    (rot,) = query_call(functools.partial(query_kernel, True), in_specs=[VMEM] + [HELD] * 4, args=(query_grads, *slabs[:4]), held=False)
    (rot,) = query_call(
        functools.partial(query_kernel, False),
        in_specs=[VMEM] * 2 + [HELD] * 4,
        args=(query_grads, rot, *slabs[4:]),
        held=False,
    )
    rot = exchange(rot.reshape(32, 4, 8, queries), ZX)
    (precond,) = call(
        precond_kernel,
        [((32, 8, 128), f32)],
        [VMEM] + [HELD] * 5,
        me, args=(eigenvalues, rot, *blocks),
        scratch=[pltpu.VMEM((queries, 128), f32)],
    )
    preconds = [precond]
    for k in (1, 2, 3):
        preconds.append(shifted(precond, "y", k))
    preconds = preconds + [shifted(p, "core", 1) for p in preconds]

    block_shape, sum_shape = ((8, 32, 512), f32), ((2, 512, HALF), bf16)
    sent = [None] * 4
    sent[2], high, low = call(
        train_kernel,
        [block_shape, sum_shape, sum_shape],
        [
            SMEM,
            pl.BlockSpec((512, out_grads.shape[1]), lambda i, me: (lax.rem(me[0] % 4 + 4 - jnp.minimum(i, 3), 4), 0)),
            *[HELD] * 12,
        ],
        me,
        args=(doc_lengths, out_grads, *blocks, *slabs),
        grid=5,
        scratch=[pltpu.VMEM((4, 128, out_grads.shape[1]), f32)],
    )
    sent[1], sent[3] = call(
        functools.partial(product_kernel, (1, 3)), [block_shape] * 2, [HELD] * 10, me, args=(high, low, *slabs)
    )
    sent[2] = shifted(sent[2], "x", 2)
    (sent[0],) = call(
        functools.partial(product_kernel, (0,)), [block_shape], [HELD] * 10, me, args=(high, low, *slabs), held=False
    )
    for k in (1, 3):
        sent[k] = shifted(sent[k], "x", k)
    train = sent[0] + sent[1] + sent[2] + sent[3]
    train = exchange(train, "z")

    (partial_scores,) = call(score_kernel, [((32, 8, 128), f32)], [HELD] * 9, me, args=(train, *preconds))
    return jnp.sum(exchange(partial_scores, ZX), axis=(0, 2)).reshape(2, 4)


def solution(mesh):
    fine = Mesh(mesh.devices.reshape(4, 2, 8, 4), ("y", "core", "z", "x"))
    seq, factor = ("y", "core"), ("z", "x")
    in_specs = (
        P(seq, factor),
        P(seq, factor),
        P(seq, factor),
        P(seq, factor),
        P(factor, None),
        P(),
        P(factor, None),
        P(seq),
        P(seq),
    )

    return jax.shard_map(local, mesh=fine, in_specs=in_specs, out_specs=P(factor, seq), check_vma=False)
```

```python
import functools

import jax
import jax.numpy as jnp
from jax import lax
from jax.experimental import pallas as pl
from jax.experimental.pallas import tpu as pltpu
from jax.sharding import Mesh, PartitionSpec as P


QLEN = 32
DAMPING = 1.0
ZX = ("z", "x")

HALF = 512
VMEM = pl.BlockSpec(memory_space=pltpu.VMEM)
HELD = pl.BlockSpec(memory_space=pltpu.VMEM)
SMEM = pl.BlockSpec(memory_space=pltpu.SMEM)
ANY = pl.BlockSpec(memory_space=pl.ANY)


def exchange(blocks, axis):
    return lax.all_to_all(blocks, axis, 0, 0, tiled=True)


def shifted(shard, axis, hops):
    n = lax.axis_size(axis)
    return lax.ppermute(shard, axis, [(i, (i + hops) % n) for i in range(n)])


def call(kernel, outs, in_specs, me, *, args, grid=1, scratch=(), held=True):
    out_shape = [(pltpu.VMEM if held else pltpu.HBM)(*o) for o in outs]
    spaces = [pltpu.VMEM if spec is HELD else None if spec is SMEM else pltpu.HBM for spec in in_specs]
    args = [a if space is None else pltpu.with_memory_space_constraint(a, space) for a, space in zip(args, spaces)]
    return pl.pallas_call(
        kernel,
        out_shape=out_shape,
        grid_spec=pltpu.PrefetchScalarGridSpec(
            num_scalar_prefetch=1,
            grid=(grid,),
            in_specs=in_specs,
            out_specs=[VMEM] * len(out_shape),
            scratch_shapes=list(scratch),
        ),
        compiler_params=pltpu.CompilerParams(vmem_limit_bytes=28 << 20),
    )(me, *args)


def place(me_ref):
    me = me_ref[0]
    return me // 64, (me // 32) % 2, (me // 4) % 8, me % 4


def split(value):
    high = value.astype(jnp.bfloat16)
    return high, (value - high.astype(jnp.float32)).astype(jnp.bfloat16)


def dot_nt(left, right):
    return lax.dot_general(
        left, right, (((1,), (1,)), ((), ())), preferred_element_type=jnp.float32
    )


def dot_nn(left, right):
    return lax.dot_general(
        left, right, (((1,), (0,)), ((), ())), preferred_element_type=jnp.float32
    )


def input_rotation_kernel(me_ref, acts_ref, query_ref, basis_ref, *out_refs):
    _, _, _, x = place(me_ref)
    high, low = split(basis_ref[...])
    for k, out_ref in enumerate(out_refs):
        target = lax.rem(x + k, 4)
        acts = acts_ref[pl.ds(pl.multiple_of(target * 512, 512), 512), :]
        query = query_ref[pl.ds(pl.multiple_of(target * 64, 64), 64), :]
        out_ref[:, :64, :] = (dot_nt(acts, high) + dot_nt(acts, low)).reshape(8, 64, 128)
        out_ref[:, 64:, :] = (dot_nt(query, high) + dot_nt(query, low)).reshape(8, 8, 128)


def basis_pick_kernel(me_ref, basis_ref, out_ref, sems):
    y, core, _, _ = place(me_ref)
    cols = basis_ref.shape[1] // 32
    rows = pl.ds(pl.multiple_of(8 * y, 8), 8)
    copies = []
    for f in range(32):
        start = pl.multiple_of(f * cols + core * (cols - HALF), 128)
        copies.append(pltpu.make_async_copy(basis_ref.at[rows, pl.ds(start, HALF)], out_ref.at[f], sems.at[f]))
        copies[-1].start()
    for copy in copies:
        copy.wait()


def query_kernel(own, me_ref, grads_ref, *refs):
    so_far = None if own else refs[0]
    slabs, out_ref, half_ref = refs[-6:-2], refs[-2], refs[-1]
    _, core, _, _ = place(me_ref)
    cols = grads_ref.shape[1]
    half = core if own else 1 - core

    @pl.when(half == 0)
    def _():
        half_ref[...] = grads_ref[:, :HALF]

    @pl.when(half == 1)
    def _():
        half_ref[:, : 2 * HALF - cols] = jnp.zeros((grads_ref.shape[0], 2 * HALF - cols), jnp.bfloat16)
        half_ref[:, 2 * HALF - cols :] = grads_ref[:, HALF:]

    for slot in range(4):
        high, low = split(slabs[slot][...].reshape(256, HALF))
        total = (dot_nt(high, half_ref[...]) + dot_nt(low, half_ref[...])).reshape(8, 4, 8, half_ref.shape[0])
        out_ref[:, :, slot] = total if own else so_far[:, :, slot] + total


def precond_kernel(me_ref, eig_ref, *refs):
    parts_ref, blocks, out_ref, rot_in_ref = refs[0], refs[1:5], refs[5], refs[6]
    y, _, _, x = place(me_ref)
    for k in range(4):
        source = lax.rem(x + 4 - k, 4)
        rot_in_ref[pl.ds(pl.multiple_of(source * 64, 64), 64), :] = blocks[k][:, 64:, :].reshape(64, 128)
    rot = parts_ref[0]
    for sender in range(1, 32):
        rot = rot + parts_ref[sender]
    rot = rot.reshape(32, rot.shape[-1])
    lane_query = lax.broadcasted_iota(jnp.int32, rot.shape, 1) // QLEN
    count = rot.shape[1] // QLEN
    masked = jnp.concatenate([jnp.where(lane_query == q, rot, 0.0) for q in range(count)], 0)
    both = lax.dot_general(
        masked,
        rot_in_ref[...],
        (((1,), (0,)), ((), ())),
        precision=lax.Precision.HIGHEST,
        preferred_element_type=jnp.float32,
    ) * (1.0 / QLEN)
    for slot in range(4):
        rows = pl.ds(pl.multiple_of(8 * lax.rem(y + slot, 4), 8), 8)
        eig = eig_ref[rows, :] + DAMPING
        for q in range(count):
            out_ref[rows, q, :] = both[32 * q + 8 * slot : 32 * q + 8 * slot + 8] / eig


def basis_product(me_ref, hops, slabs, high_ref, low_ref, out_ref):
    _, core, _, x = place(me_ref)
    target = lax.rem(x + hops, 4)
    total = None
    for half, group in ((core, slabs[:4]), (1 - core, slabs[4:])):
        value = jnp.concatenate([ref[:, target].reshape(64, HALF) for ref in group], 0)
        high, low = split(value)
        part = dot_nt(high, high_ref[half]) + dot_nt(high, low_ref[half]) + dot_nt(low, high_ref[half])
        total = part if total is None else total + part
    for slot in range(4):
        out_ref[:, 8 * slot : 8 * slot + 8, :] = total[64 * slot : 64 * slot + 64].reshape(8, 8, 512)


def add_block(me_ref, len_ref, hops, grads_ref, block_ref, total_ref):
    _, _, _, x = place(me_ref)
    first = lax.rem(x + 4 - hops, 4) * 512
    high, low = split(block_ref[:, :64, :].reshape(512, 128).T)
    pair = jnp.concatenate([high, low], 0)
    token = first + lax.broadcasted_iota(jnp.int32, pair.shape, 1)
    begin = jnp.int32(0)
    for doc in range(4):
        end = begin + len_ref[doc]

        @pl.when((begin < first + 512) & (end > first))
        def _(begin=begin, end=end, doc=doc):
            masked = jnp.where((token >= begin) & (token < end), pair, jnp.zeros_like(pair))
            both = dot_nn(masked, grads_ref[...])
            total_ref[doc] += both[:128] + both[128:]

        begin = end


def outer_own_kernel(me_ref, len_ref, grads_ref, block_ref, total_ref):
    total_ref[...] = jnp.zeros_like(total_ref)
    add_block(me_ref, len_ref, 0, grads_ref, block_ref, total_ref)


def outer_side_kernel(me_ref, len_ref, grads_ref, ahead_ref, behind_ref, so_far_ref, total_ref):
    @pl.when(pl.program_id(0) == 0)
    def _():
        total_ref[...] = so_far_ref[...]
        add_block(me_ref, len_ref, 1, grads_ref, ahead_ref, total_ref)

    @pl.when(pl.program_id(0) == 1)
    def _():
        add_block(me_ref, len_ref, 3, grads_ref, behind_ref, total_ref)


def train_kernel(me_ref, len_ref, grads_ref, block_ref, so_far_ref, *refs):
    slabs, (out_ref, high_ref, low_ref, total_ref) = refs[:8], refs[8:]
    cols = grads_ref.shape[1]
    total_ref[...] = so_far_ref[...]
    add_block(me_ref, len_ref, 2, grads_ref, block_ref, total_ref)
    for doc in range(4):
        length = jnp.full((128, cols), len_ref[doc], jnp.int32).astype(jnp.float32)
        high, low = split(total_ref[doc] / length)
        rows = slice(128 * doc, 128 * doc + 128)
        for ref, value in ((high_ref, high), (low_ref, low)):
            ref[0, rows, :] = value[:, :HALF]
            ref[1, rows, : 2 * HALF - cols] = jnp.zeros((128, 2 * HALF - cols), jnp.bfloat16)
            ref[1, rows, 2 * HALF - cols :] = value[:, HALF:]
    basis_product(me_ref, 2, slabs, high_ref, low_ref, out_ref)


def product_kernel(hops, me_ref, high_ref, low_ref, *refs):
    slabs, out_refs = refs[:8], refs[8:]
    for k, out_ref in zip(hops, out_refs):
        basis_product(me_ref, k, slabs, high_ref, low_ref, out_ref)


def score_kernel(me_ref, blocks_ref, *refs):
    preconds, out_ref = refs[:8], refs[8]
    y, core, _, _ = place(me_ref)
    train = blocks_ref[0]
    for sender in range(1, 8):
        train = train + blocks_ref[sender]
    for index, ref in enumerate(preconds):
        other, k = divmod(index, 4)
        owner = 2 * lax.rem(y + 4 - k, 4) + lax.rem(core + other, 2)
        sums = [None] * 4
        for slot in range(4):
            base = 8 * lax.rem(y + slot, 4)
            for r in range(8):
                value = ref[base + r]
                row = train[8 * slot + r : 8 * slot + r + 1]
                for doc in range(4):
                    product = value * row[:, 128 * doc : 128 * doc + 128]
                    sums[doc] = product if sums[doc] is None else sums[doc] + product
        for q in range(8):
            for doc in range(4):
                out_ref[4 * owner + q // 2, 4 * (q % 2) + doc : 4 * (q % 2) + doc + 1, :] = sums[doc][q : q + 1]


def local(
    out_grads,
    in_acts,
    query_grads,
    query_acts,
    output_basis,
    input_basis,
    eigenvalues,
    doc_ids,
    doc_lengths,
):
    f32, bf16 = jnp.float32, jnp.bfloat16
    me = lax.axis_index(("y", "core", "z", "x")).astype(jnp.int32).reshape(1)
    queries = query_grads.shape[0]

    parts = call(
        input_rotation_kernel,
        [((8, 72, 128), f32)] * 4,
        [VMEM, VMEM, pl.BlockSpec((128, in_acts.shape[1]), lambda i, me: (0, me[0] % 32))],
        me, args=(in_acts, query_acts, input_basis),
    )
    arrived = [parts[0]]
    for k in (2, 1, 3):
        arrived.append(shifted(parts[k], "x", k))
    part = arrived[0] + arrived[1] + arrived[2] + arrived[3]
    part = exchange(part, "z")
    part = jnp.broadcast_to(jnp.sum(part, axis=0)[None], (8, 72, 128))
    block = exchange(part, "z")
    blocks = [block] + [None] * 3
    for k in (2, 1, 3):
        blocks[k] = shifted(block, "x", k)

    (picked,) = call(
        basis_pick_kernel,
        [((32, 8, HALF), f32)],
        [ANY],
        me, args=(output_basis,), held=False,
        scratch=[pltpu.SemaphoreType.DMA((32,))],
    )
    slab = exchange(picked, ZX).reshape(8, 4, 8, HALF)
    slabs = [slab]
    for k in (1, 2, 3):
        slabs.append(shifted(slab, "y", 4 - k))
    for k in range(4):
        slabs.append(shifted(slabs[k], "core", 1))

    query_call = functools.partial(
        call, outs=[((8, 4, 4, 8, queries), f32)], me=me, scratch=[pltpu.VMEM((queries, HALF), bf16)]
    )
    (rot,) = query_call(functools.partial(query_kernel, True), in_specs=[VMEM] + [HELD] * 4, args=(query_grads, *slabs[:4]))
    (rot,) = query_call(
        functools.partial(query_kernel, False),
        in_specs=[VMEM] + [HELD] * 5,
        args=(query_grads, rot, *slabs[4:]),
        held=False,
    )
    rot = exchange(rot.reshape(32, 4, 8, queries), ZX)
    (precond,) = call(
        precond_kernel,
        [((32, 8, 128), f32)],
        [VMEM] + [HELD] * 5,
        me, args=(eigenvalues, rot, *blocks),
        scratch=[pltpu.VMEM((queries, 128), f32)],
    )
    preconds = [precond]
    for k in (1, 2, 3):
        preconds.append(shifted(precond, "y", k))
    preconds = preconds + [shifted(p, "core", 1) for p in preconds]

    block_shape, sum_shape = ((8, 32, 512), f32), ((2, 512, HALF), bf16)
    sent = [None] * 4
    total_shape = ((4, 128, out_grads.shape[1]), f32)

    def grads_spec(first, stride=0):
        return pl.BlockSpec(
            (512, out_grads.shape[1]), lambda i, me: (lax.rem(me[0] % 4 + 4 - first - stride * i, 4), 0)
        )

    (total,) = call(
        outer_own_kernel,
        [total_shape],
        [SMEM, grads_spec(0), HELD],
        me, args=(doc_lengths, out_grads, blocks[0]), held=False,
    )
    (total,) = call(
        outer_side_kernel,
        [total_shape],
        [SMEM, grads_spec(1, 2), HELD, HELD, VMEM],
        me, args=(doc_lengths, out_grads, blocks[1], blocks[3], total),
        grid=2,
    )
    sent[2], high, low = call(
        train_kernel,
        [block_shape, sum_shape, sum_shape],
        [SMEM, grads_spec(2), *[HELD] * 10],
        me, args=(doc_lengths, out_grads, blocks[2], total, *slabs),
        scratch=[pltpu.VMEM(*total_shape)],
    )
    sent[1], sent[3] = call(
        functools.partial(product_kernel, (1, 3)), [block_shape] * 2, [HELD] * 10, me, args=(high, low, *slabs)
    )
    sent[2] = shifted(sent[2], "x", 2)
    (sent[0],) = call(
        functools.partial(product_kernel, (0,)), [block_shape], [HELD] * 10, me, args=(high, low, *slabs), held=False
    )
    for k in (1, 3):
        sent[k] = shifted(sent[k], "x", k)
    train = sent[0] + sent[1] + sent[2] + sent[3]
    train = exchange(train, "z")

    (partial_scores,) = call(score_kernel, [((32, 8, 128), f32)], [HELD] * 9, me, args=(train, *preconds))
    return jnp.sum(exchange(partial_scores, ZX), axis=(0, 2)).reshape(2, 4)


def solution(mesh):
    fine = Mesh(mesh.devices.reshape(4, 2, 8, 4), ("y", "core", "z", "x"))
    seq, factor = ("y", "core"), ("z", "x")
    in_specs = (
        P(seq, factor),
        P(seq, factor),
        P(seq, factor),
        P(seq, factor),
        P(factor, None),
        P(),
        P(factor, None),
        P(seq),
        P(seq),
    )

    return jax.shard_map(local, mesh=fine, in_specs=in_specs, out_specs=P(factor, seq), check_vma=False)
```

```python
import functools

import jax
import jax.numpy as jnp
from jax import lax
from jax.experimental import pallas as pl
from jax.experimental.pallas import tpu as pltpu
from jax.sharding import Mesh, PartitionSpec as P


QLEN = 32
DAMPING = 1.0
ZX = ("z", "x")

HALF = 512
VMEM = pl.BlockSpec(memory_space=pltpu.VMEM)
HELD = pl.BlockSpec(memory_space=pltpu.VMEM)
SMEM = pl.BlockSpec(memory_space=pltpu.SMEM)
ANY = pl.BlockSpec(memory_space=pl.ANY)


def exchange(blocks, axis):
    return lax.all_to_all(blocks, axis, 0, 0, tiled=True)


def shifted(shard, axis, hops):
    n = lax.axis_size(axis)
    return lax.ppermute(shard, axis, [(i, (i + hops) % n) for i in range(n)])


def call(kernel, outs, in_specs, me, *, args, grid=1, scratch=(), held=True):
    out_shape = [(pltpu.VMEM if held else pltpu.HBM)(*o) for o in outs]
    spaces = [pltpu.VMEM if spec is HELD else None if spec is SMEM else pltpu.HBM for spec in in_specs]
    args = [a if space is None else pltpu.with_memory_space_constraint(a, space) for a, space in zip(args, spaces)]
    return pl.pallas_call(
        kernel,
        out_shape=out_shape,
        grid_spec=pltpu.PrefetchScalarGridSpec(
            num_scalar_prefetch=1,
            grid=(grid,),
            in_specs=in_specs,
            out_specs=[VMEM] * len(out_shape),
            scratch_shapes=list(scratch),
        ),
        compiler_params=pltpu.CompilerParams(vmem_limit_bytes=28 << 20),
    )(me, *args)


def place(me_ref):
    me = me_ref[0]
    return me // 64, (me // 32) % 2, (me // 4) % 8, me % 4


def split(value):
    high = value.astype(jnp.bfloat16)
    return high, (value - high.astype(jnp.float32)).astype(jnp.bfloat16)


def dot_nt(left, right):
    return lax.dot_general(
        left, right, (((1,), (1,)), ((), ())), preferred_element_type=jnp.float32
    )


def dot_nn(left, right):
    return lax.dot_general(
        left, right, (((1,), (0,)), ((), ())), preferred_element_type=jnp.float32
    )


def input_rotation_kernel(me_ref, acts_ref, query_ref, basis_ref, *out_refs):
    _, _, _, x = place(me_ref)
    high, low = split(basis_ref[...])
    for k, out_ref in enumerate(out_refs):
        target = lax.rem(x + k, 4)
        acts = acts_ref[pl.ds(pl.multiple_of(target * 512, 512), 512), :]
        query = query_ref[pl.ds(pl.multiple_of(target * 64, 64), 64), :]
        out_ref[:, :64, :] = (dot_nt(acts, high) + dot_nt(acts, low)).reshape(8, 64, 128)
        out_ref[:, 64:, :] = (dot_nt(query, high) + dot_nt(query, low)).reshape(8, 8, 128)


def basis_pick_kernel(me_ref, basis_ref, out_ref, sems):
    y, core, _, _ = place(me_ref)
    cols = basis_ref.shape[1] // 32
    rows = pl.ds(pl.multiple_of(8 * y, 8), 8)
    copies = []
    for f in range(32):
        start = pl.multiple_of(f * cols + core * (cols - HALF), 128)
        copies.append(pltpu.make_async_copy(basis_ref.at[rows, pl.ds(start, HALF)], out_ref.at[f], sems.at[f]))
        copies[-1].start()
    for copy in copies:
        copy.wait()


def query_kernel(own, me_ref, grads_ref, *refs):
    so_far = None if own else refs[0]
    slabs, out_ref, half_ref = refs[-6:-2], refs[-2], refs[-1]
    _, core, _, _ = place(me_ref)
    cols = grads_ref.shape[1]
    half = core if own else 1 - core

    @pl.when(half == 0)
    def _():
        half_ref[...] = grads_ref[:, :HALF]

    @pl.when(half == 1)
    def _():
        half_ref[:, : 2 * HALF - cols] = jnp.zeros((grads_ref.shape[0], 2 * HALF - cols), jnp.bfloat16)
        half_ref[:, 2 * HALF - cols :] = grads_ref[:, HALF:]

    for slot in range(4):
        high, low = split(slabs[slot][...].reshape(256, HALF))
        total = (dot_nt(high, half_ref[...]) + dot_nt(low, half_ref[...])).reshape(8, 4, 8, half_ref.shape[0])
        out_ref[:, :, slot] = total if own else so_far[:, :, slot] + total


def query_sum_kernel(me_ref, blocks_ref, *out_refs):
    _, _, _, x = place(me_ref)
    for k, out_ref in enumerate(out_refs):
        target = lax.rem(x + k, 4)
        total = blocks_ref[0, target]
        for sender in range(1, 8):
            total = total + blocks_ref[sender, target]
        out_ref[...] = total


def precond_kernel(me_ref, eig_ref, *refs):
    parts, blocks, out_ref, rot_in_ref = refs[:4], refs[4:8], refs[8], refs[9]
    y, _, _, x = place(me_ref)
    for k in range(4):
        source = lax.rem(x + 4 - k, 4)
        rot_in_ref[pl.ds(pl.multiple_of(source * 64, 64), 64), :] = blocks[k][:, 64:, :].reshape(64, 128)
    rot = parts[0][...] + parts[1][...] + parts[2][...] + parts[3][...]
    rot = rot.reshape(32, rot.shape[-1])
    lane_query = lax.broadcasted_iota(jnp.int32, rot.shape, 1) // QLEN
    count = rot.shape[1] // QLEN
    masked = jnp.concatenate([jnp.where(lane_query == q, rot, 0.0) for q in range(count)], 0)
    both = lax.dot_general(
        masked,
        rot_in_ref[...],
        (((1,), (0,)), ((), ())),
        precision=lax.Precision.HIGHEST,
        preferred_element_type=jnp.float32,
    ) * (1.0 / QLEN)
    for slot in range(4):
        rows = pl.ds(pl.multiple_of(8 * lax.rem(y + slot, 4), 8), 8)
        eig = eig_ref[rows, :] + DAMPING
        for q in range(count):
            out_ref[rows, q, :] = both[32 * q + 8 * slot : 32 * q + 8 * slot + 8] / eig


def basis_product(me_ref, hops, slabs, high_ref, low_ref, out_ref):
    _, core, _, x = place(me_ref)
    target = lax.rem(x + hops, 4)
    total = None
    for half, group in ((core, slabs[:4]), (1 - core, slabs[4:])):
        value = jnp.concatenate([ref[:, target].reshape(64, HALF) for ref in group], 0)
        high, low = split(value)
        part = dot_nt(high, high_ref[half]) + dot_nt(high, low_ref[half]) + dot_nt(low, high_ref[half])
        total = part if total is None else total + part
    for slot in range(4):
        out_ref[:, 8 * slot : 8 * slot + 8, :] = total[64 * slot : 64 * slot + 64].reshape(8, 8, 512)


def add_block(me_ref, len_ref, hops, grads_ref, block_ref, total_ref):
    _, _, _, x = place(me_ref)
    first = lax.rem(x + 4 - hops, 4) * 512
    high, low = split(block_ref[:, :64, :].reshape(512, 128).T)
    pair = jnp.concatenate([high, low], 0)
    token = first + lax.broadcasted_iota(jnp.int32, pair.shape, 1)
    begin = jnp.int32(0)
    for doc in range(4):
        end = begin + len_ref[doc]

        @pl.when((begin < first + 512) & (end > first))
        def _(begin=begin, end=end, doc=doc):
            masked = jnp.where((token >= begin) & (token < end), pair, jnp.zeros_like(pair))
            both = dot_nn(masked, grads_ref[...])
            total_ref[doc] += both[:128] + both[128:]

        begin = end


def outer_own_kernel(me_ref, len_ref, grads_ref, block_ref, total_ref):
    total_ref[...] = jnp.zeros_like(total_ref)
    add_block(me_ref, len_ref, 0, grads_ref, block_ref, total_ref)


def outer_side_kernel(me_ref, len_ref, grads_ref, ahead_ref, behind_ref, so_far_ref, total_ref):
    @pl.when(pl.program_id(0) == 0)
    def _():
        total_ref[...] = so_far_ref[...]
        add_block(me_ref, len_ref, 1, grads_ref, ahead_ref, total_ref)

    @pl.when(pl.program_id(0) == 1)
    def _():
        add_block(me_ref, len_ref, 3, grads_ref, behind_ref, total_ref)


def train_kernel(me_ref, len_ref, grads_ref, block_ref, so_far_ref, *refs):
    slabs, (out_ref, high_ref, low_ref, total_ref) = refs[:8], refs[8:]
    cols = grads_ref.shape[1]
    total_ref[...] = so_far_ref[...]
    add_block(me_ref, len_ref, 2, grads_ref, block_ref, total_ref)
    for doc in range(4):
        length = jnp.full((128, cols), len_ref[doc], jnp.int32).astype(jnp.float32)
        high, low = split(total_ref[doc] / length)
        rows = slice(128 * doc, 128 * doc + 128)
        for ref, value in ((high_ref, high), (low_ref, low)):
            ref[0, rows, :] = value[:, :HALF]
            ref[1, rows, : 2 * HALF - cols] = jnp.zeros((128, 2 * HALF - cols), jnp.bfloat16)
            ref[1, rows, 2 * HALF - cols :] = value[:, HALF:]
    basis_product(me_ref, 2, slabs, high_ref, low_ref, out_ref)


def product_kernel(hops, me_ref, high_ref, low_ref, *refs):
    slabs, out_refs = refs[:8], refs[8:]
    for k, out_ref in zip(hops, out_refs):
        basis_product(me_ref, k, slabs, high_ref, low_ref, out_ref)


def score_kernel(me_ref, blocks_ref, *refs):
    preconds, out_ref = refs[:8], refs[8]
    y, core, _, _ = place(me_ref)
    train = blocks_ref[0]
    for sender in range(1, 8):
        train = train + blocks_ref[sender]
    for index, ref in enumerate(preconds):
        other, k = divmod(index, 4)
        owner = 2 * lax.rem(y + 4 - k, 4) + lax.rem(core + other, 2)
        sums = [None] * 4
        for slot in range(4):
            base = 8 * lax.rem(y + slot, 4)
            for r in range(8):
                value = ref[base + r]
                row = train[8 * slot + r : 8 * slot + r + 1]
                for doc in range(4):
                    product = value * row[:, 128 * doc : 128 * doc + 128]
                    sums[doc] = product if sums[doc] is None else sums[doc] + product
        for q in range(8):
            for doc in range(4):
                out_ref[4 * owner + q // 2, 4 * (q % 2) + doc : 4 * (q % 2) + doc + 1, :] = sums[doc][q : q + 1]


def local(
    out_grads,
    in_acts,
    query_grads,
    query_acts,
    output_basis,
    input_basis,
    eigenvalues,
    doc_ids,
    doc_lengths,
):
    f32, bf16 = jnp.float32, jnp.bfloat16
    me = lax.axis_index(("y", "core", "z", "x")).astype(jnp.int32).reshape(1)
    queries = query_grads.shape[0]

    parts = call(
        input_rotation_kernel,
        [((8, 72, 128), f32)] * 4,
        [VMEM, VMEM, pl.BlockSpec((128, in_acts.shape[1]), lambda i, me: (0, me[0] % 32))],
        me, args=(in_acts, query_acts, input_basis),
    )
    arrived = [parts[0]]
    for k in (2, 1, 3):
        arrived.append(shifted(parts[k], "x", k))
    part = arrived[0] + arrived[1] + arrived[2] + arrived[3]
    part = exchange(part, "z")
    part = jnp.broadcast_to(jnp.sum(part, axis=0)[None], (8, 72, 128))
    block = exchange(part, "z")
    blocks = [block] + [None] * 3
    for k in (2, 1, 3):
        blocks[k] = shifted(block, "x", k)

    (picked,) = call(
        basis_pick_kernel,
        [((32, 8, HALF), f32)],
        [ANY],
        me, args=(output_basis,), held=False,
        scratch=[pltpu.SemaphoreType.DMA((32,))],
    )
    slab = exchange(picked, ZX).reshape(8, 4, 8, HALF)
    slabs = [slab]
    for k in (1, 2, 3):
        slabs.append(shifted(slab, "y", 4 - k))
    for k in range(4):
        slabs.append(shifted(slabs[k], "core", 1))

    query_call = functools.partial(
        call, outs=[((8, 4, 4, 8, queries), f32)], me=me, scratch=[pltpu.VMEM((queries, HALF), bf16)]
    )
    (rot,) = query_call(functools.partial(query_kernel, True), in_specs=[VMEM] + [HELD] * 4, args=(query_grads, *slabs[:4]))
    (rot,) = query_call(
        functools.partial(query_kernel, False),
        in_specs=[VMEM] + [HELD] * 5,
        args=(query_grads, rot, *slabs[4:]),
        held=False,
    )
    rot = exchange(rot, "z")
    rots = call(query_sum_kernel, [((4, 8, queries), f32)] * 4, [HELD], me, args=(rot,))
    rots = [rots[0], *rots[1:]]
    for k in (1, 2, 3):
        rots[k] = shifted(rots[k], "x", k)
    (precond,) = call(
        precond_kernel,
        [((32, 8, 128), f32)],
        [VMEM] + [HELD] * 8,
        me, args=(eigenvalues, *rots, *blocks),
        scratch=[pltpu.VMEM((queries, 128), f32)],
    )
    preconds = [precond]
    for k in (1, 2, 3):
        preconds.append(shifted(precond, "y", k))
    preconds = preconds + [shifted(p, "core", 1) for p in preconds]

    block_shape, sum_shape = ((8, 32, 512), f32), ((2, 512, HALF), bf16)
    sent = [None] * 4
    total_shape = ((4, 128, out_grads.shape[1]), f32)

    def grads_spec(first, stride=0):
        return pl.BlockSpec(
            (512, out_grads.shape[1]), lambda i, me: (lax.rem(me[0] % 4 + 4 - first - stride * i, 4), 0)
        )

    (total,) = call(
        outer_own_kernel,
        [total_shape],
        [SMEM, grads_spec(0), HELD],
        me, args=(doc_lengths, out_grads, blocks[0]), held=False,
    )
    (total,) = call(
        outer_side_kernel,
        [total_shape],
        [SMEM, grads_spec(1, 2), HELD, HELD, VMEM],
        me, args=(doc_lengths, out_grads, blocks[1], blocks[3], total),
        grid=2,
    )
    sent[2], high, low = call(
        train_kernel,
        [block_shape, sum_shape, sum_shape],
        [SMEM, grads_spec(2), *[HELD] * 10],
        me, args=(doc_lengths, out_grads, blocks[2], total, *slabs),
        scratch=[pltpu.VMEM(*total_shape)],
    )
    sent[1], sent[3] = call(
        functools.partial(product_kernel, (1, 3)), [block_shape] * 2, [HELD] * 10, me, args=(high, low, *slabs)
    )
    sent[2] = shifted(sent[2], "x", 2)
    (sent[0],) = call(
        functools.partial(product_kernel, (0,)), [block_shape], [HELD] * 10, me, args=(high, low, *slabs), held=False
    )
    for k in (1, 3):
        sent[k] = shifted(sent[k], "x", k)
    train = sent[0] + sent[1] + sent[2] + sent[3]
    train = exchange(train, "z")

    (partial_scores,) = call(score_kernel, [((32, 8, 128), f32)], [HELD] * 9, me, args=(train, *preconds))
    return jnp.sum(exchange(partial_scores, ZX), axis=(0, 2)).reshape(2, 4)


def solution(mesh):
    fine = Mesh(mesh.devices.reshape(4, 2, 8, 4), ("y", "core", "z", "x"))
    seq, factor = ("y", "core"), ("z", "x")
    in_specs = (
        P(seq, factor),
        P(seq, factor),
        P(seq, factor),
        P(seq, factor),
        P(factor, None),
        P(),
        P(factor, None),
        P(seq),
        P(seq),
    )

    return jax.shard_map(local, mesh=fine, in_specs=in_specs, out_specs=P(factor, seq), check_vma=False)
```

```python
import functools

import jax
import jax.numpy as jnp
from jax import lax
from jax.experimental import pallas as pl
from jax.experimental.pallas import tpu as pltpu
from jax.sharding import Mesh, PartitionSpec as P


QLEN = 32
DAMPING = 1.0
ZX = ("z", "x")

HALF = 512
VMEM = pl.BlockSpec(memory_space=pltpu.VMEM)
HELD = pl.BlockSpec(memory_space=pltpu.VMEM)
SMEM = pl.BlockSpec(memory_space=pltpu.SMEM)
ANY = pl.BlockSpec(memory_space=pl.ANY)


def exchange(blocks, axis):
    return lax.all_to_all(blocks, axis, 0, 0, tiled=True)


def shifted(shard, axis, hops):
    n = lax.axis_size(axis)
    return lax.ppermute(shard, axis, [(i, (i + hops) % n) for i in range(n)])


def call(kernel, outs, in_specs, me, *, args, grid=1, scratch=(), held=True, out_spec=VMEM):
    out_shape = [(pltpu.VMEM if held else pltpu.HBM)(*o) for o in outs]
    spaces = [pltpu.VMEM if spec is HELD else None if spec is SMEM else pltpu.HBM for spec in in_specs]
    args = [a if space is None else pltpu.with_memory_space_constraint(a, space) for a, space in zip(args, spaces)]
    return pl.pallas_call(
        kernel,
        out_shape=out_shape,
        grid_spec=pltpu.PrefetchScalarGridSpec(
            num_scalar_prefetch=1,
            grid=(grid,),
            in_specs=in_specs,
            out_specs=[out_spec] * len(out_shape),
            scratch_shapes=list(scratch),
        ),
        compiler_params=pltpu.CompilerParams(vmem_limit_bytes=28 << 20),
    )(me, *args)


def place(me_ref):
    me = me_ref[0]
    return me // 64, (me // 32) % 2, (me // 4) % 8, me % 4


def split(value):
    high = value.astype(jnp.bfloat16)
    return high, (value - high.astype(jnp.float32)).astype(jnp.bfloat16)


def dot_nt(left, right):
    return lax.dot_general(
        left, right, (((1,), (1,)), ((), ())), preferred_element_type=jnp.float32
    )


def dot_nn(left, right):
    return lax.dot_general(
        left, right, (((1,), (0,)), ((), ())), preferred_element_type=jnp.float32
    )


def input_rotation_kernel(me_ref, acts_ref, query_ref, basis_ref, *out_refs):
    _, _, _, x = place(me_ref)
    high, low = split(basis_ref[...])
    for k, out_ref in enumerate(out_refs):
        target = lax.rem(x + k, 4)
        acts = acts_ref[pl.ds(pl.multiple_of(target * 512, 512), 512), :]
        query = query_ref[pl.ds(pl.multiple_of(target * 64, 64), 64), :]
        out_ref[:, :64, :] = (dot_nt(acts, high) + dot_nt(acts, low)).reshape(8, 64, 128)
        out_ref[:, 64:, :] = (dot_nt(query, high) + dot_nt(query, low)).reshape(8, 8, 128)


def basis_pick_kernel(me_ref, basis_ref, out_ref, sems):
    y, core, _, _ = place(me_ref)
    cols = basis_ref.shape[1] // 32
    rows = pl.ds(pl.multiple_of(8 * y, 8), 8)
    copies = []
    for f in range(32):
        start = pl.multiple_of(f * cols + core * (cols - HALF), 128)
        copies.append(pltpu.make_async_copy(basis_ref.at[rows, pl.ds(start, HALF)], out_ref.at[f], sems.at[f]))
        copies[-1].start()
    for copy in copies:
        copy.wait()


def query_kernel(own, me_ref, grads_ref, *refs):
    so_far = None if own else refs[0]
    slabs, out_ref, half_ref = refs[-6:-2], refs[-2], refs[-1]
    _, core, _, _ = place(me_ref)
    cols = grads_ref.shape[1]
    half = core if own else 1 - core

    @pl.when(half == 0)
    def _():
        half_ref[...] = grads_ref[:, :HALF]

    @pl.when(half == 1)
    def _():
        half_ref[:, : 2 * HALF - cols] = jnp.zeros((grads_ref.shape[0], 2 * HALF - cols), jnp.bfloat16)
        half_ref[:, 2 * HALF - cols :] = grads_ref[:, HALF:]

    for slot in range(4):
        high, low = split(slabs[slot][...].reshape(256, HALF))
        total = (dot_nt(high, half_ref[...]) + dot_nt(low, half_ref[...])).reshape(8, 4, 8, half_ref.shape[0])
        out_ref[:, :, slot] = total if own else so_far[:, :, slot] + total


def query_sum_kernel(me_ref, blocks_ref, *out_refs):
    _, _, _, x = place(me_ref)
    for k, out_ref in enumerate(out_refs):
        target = lax.rem(x + k, 4)
        total = blocks_ref[0, target]
        for sender in range(1, 8):
            total = total + blocks_ref[sender, target]
        out_ref[...] = total


def precond_kernel(me_ref, eig_ref, *refs):
    parts, blocks, out_ref, rot_in_ref = refs[:4], refs[4:8], refs[8], refs[9]
    y, _, _, x = place(me_ref)
    for k in range(4):
        source = lax.rem(x + 4 - k, 4)
        rot_in_ref[pl.ds(pl.multiple_of(source * 64, 64), 64), :] = blocks[k][:, 64:, :].reshape(64, 128)
    rot = parts[0][...] + parts[1][...] + parts[2][...] + parts[3][...]
    rot = rot.reshape(32, rot.shape[-1])
    lane_query = lax.broadcasted_iota(jnp.int32, rot.shape, 1) // QLEN
    count = rot.shape[1] // QLEN
    masked = jnp.concatenate([jnp.where(lane_query == q, rot, 0.0) for q in range(count)], 0)
    both = lax.dot_general(
        masked,
        rot_in_ref[...],
        (((1,), (0,)), ((), ())),
        precision=lax.Precision.HIGHEST,
        preferred_element_type=jnp.float32,
    ) * (1.0 / QLEN)
    for slot in range(4):
        rows = pl.ds(pl.multiple_of(8 * lax.rem(y + slot, 4), 8), 8)
        eig = eig_ref[rows, :] + DAMPING
        for q in range(count):
            out_ref[rows, q, :] = both[32 * q + 8 * slot : 32 * q + 8 * slot + 8] / eig


def basis_product(me_ref, hops, slabs, high_ref, low_ref, out_ref):
    _, core, _, x = place(me_ref)
    target = lax.rem(x + hops, 4)
    total = None
    for half, group in ((core, slabs[:4]), (1 - core, slabs[4:])):
        value = jnp.concatenate([ref[:, target].reshape(64, HALF) for ref in group], 0)
        high, low = split(value)
        part = dot_nt(high, high_ref[half]) + dot_nt(high, low_ref[half]) + dot_nt(low, high_ref[half])
        total = part if total is None else total + part
    for slot in range(4):
        out_ref[:, 8 * slot : 8 * slot + 8, :] = total[64 * slot : 64 * slot + 64].reshape(8, 8, 512)


def add_block(me_ref, len_ref, hops, grads_ref, block_ref, total_ref):
    _, _, _, x = place(me_ref)
    first = lax.rem(x + 4 - hops, 4) * 512
    high, low = split(block_ref[:, :64, :].reshape(512, 128).T)
    pair = jnp.concatenate([high, low], 0)
    for part in (0, 256):
        half = pair[:, part : part + 256]
        token = first + part + lax.broadcasted_iota(jnp.int32, half.shape, 1)
        begin = jnp.int32(0)
        for doc in range(4):
            end = begin + len_ref[doc]

            @pl.when((begin < first + part + 256) & (end > first + part))
            def _(begin=begin, end=end, doc=doc, part=part, half=half, token=token):
                masked = jnp.where((token >= begin) & (token < end), half, jnp.zeros_like(half))
                both = dot_nn(masked, grads_ref[part : part + 256, :])
                total_ref[doc] += both[:128] + both[128:]

            begin = end


def outer_own_kernel(me_ref, len_ref, grads_ref, block_ref, total_ref):
    total_ref[...] = jnp.zeros_like(total_ref)
    add_block(me_ref, len_ref, 0, grads_ref, block_ref, total_ref)


def outer_side_kernel(me_ref, len_ref, grads_ref, ahead_ref, behind_ref, so_far_ref, total_ref):
    @pl.when(pl.program_id(0) == 0)
    def _():
        total_ref[...] = so_far_ref[...]
        add_block(me_ref, len_ref, 1, grads_ref, ahead_ref, total_ref)

    @pl.when(pl.program_id(0) == 1)
    def _():
        add_block(me_ref, len_ref, 3, grads_ref, behind_ref, total_ref)


def train_kernel(me_ref, len_ref, grads_ref, block_ref, so_far_ref, *refs):
    slabs, (out_ref, high_ref, low_ref, total_ref) = refs[:8], refs[8:]
    cols = grads_ref.shape[1]
    total_ref[...] = so_far_ref[...]
    add_block(me_ref, len_ref, 2, grads_ref, block_ref, total_ref)
    for doc in range(4):
        length = jnp.full((128, cols), len_ref[doc], jnp.int32).astype(jnp.float32)
        high, low = split(total_ref[doc] / length)
        rows = slice(128 * doc, 128 * doc + 128)
        for ref, value in ((high_ref, high), (low_ref, low)):
            ref[0, rows, :] = value[:, :HALF]
            ref[1, rows, : 2 * HALF - cols] = jnp.zeros((128, 2 * HALF - cols), jnp.bfloat16)
            ref[1, rows, 2 * HALF - cols :] = value[:, HALF:]
    basis_product(me_ref, 2, slabs, high_ref, low_ref, out_ref)


def product_kernel(hops, me_ref, high_ref, low_ref, *refs):
    slabs, out_refs = refs[:8], refs[8:]
    for k, out_ref in zip(hops, out_refs):
        basis_product(me_ref, k, slabs, high_ref, low_ref, out_ref)


def score_kernel(me_ref, blocks_ref, *refs):
    preconds, out_ref, sums_ref = refs[:8], refs[8], refs[9]
    y, core, _, _ = place(me_ref)
    train = blocks_ref[0]
    for sender in range(1, 8):
        train = train + blocks_ref[sender]
    for index, ref in enumerate(preconds):
        other, k = divmod(index, 4)
        owner = 2 * lax.rem(y + 4 - k, 4) + lax.rem(core + other, 2)
        sums = [None] * 4
        for slot in range(4):
            base = 8 * lax.rem(y + slot, 4)
            for r in range(8):
                value = ref[base + r]
                row = train[8 * slot + r : 8 * slot + r + 1]
                for doc in range(4):
                    product = value * row[:, 128 * doc : 128 * doc + 128]
                    sums[doc] = product if sums[doc] is None else sums[doc] + product
        for doc in range(4):
            sums_ref[doc, pl.ds(pl.multiple_of(8 * owner, 8), 8), :] = sums[doc]
    lane = lax.broadcasted_iota(jnp.int32, out_ref.shape, 1)
    scores = jnp.zeros(out_ref.shape, jnp.float32)
    for doc in range(4):
        scores = jnp.where(lane == doc, jnp.sum(sums_ref[doc], axis=1, keepdims=True), scores)
    out_ref[...] = scores


def train_sum_kernel(me_ref, *refs):
    refs[4][...] = refs[0][...] + refs[1][...] + refs[2][...] + refs[3][...]


def local(
    out_grads,
    in_acts,
    query_grads,
    query_acts,
    output_basis,
    input_basis,
    eigenvalues,
    doc_ids,
    doc_lengths,
):
    f32, bf16 = jnp.float32, jnp.bfloat16
    me = lax.axis_index(("y", "core", "z", "x")).astype(jnp.int32).reshape(1)
    queries = query_grads.shape[0]

    parts = call(
        input_rotation_kernel,
        [((8, 72, 128), f32)] * 4,
        [VMEM, VMEM, pl.BlockSpec((128, in_acts.shape[1]), lambda i, me: (0, me[0] % 32))],
        me, args=(in_acts, query_acts, input_basis),
    )
    arrived = [parts[0]]
    for k in (2, 1, 3):
        arrived.append(shifted(parts[k], "x", k))
    part = arrived[0] + arrived[1] + arrived[2] + arrived[3]
    part = exchange(part, "z")
    part = jnp.broadcast_to(jnp.sum(part, axis=0)[None], (8, 72, 128))
    block = exchange(part, "z")
    blocks = [block] + [None] * 3
    for k in (2, 1, 3):
        blocks[k] = shifted(block, "x", k)

    (picked,) = call(
        basis_pick_kernel,
        [((32, 8, HALF), f32)],
        [ANY],
        me, args=(output_basis,), held=False,
        scratch=[pltpu.SemaphoreType.DMA((32,))],
    )
    slab = exchange(picked, ZX).reshape(8, 4, 8, HALF)
    slabs = [slab]
    for k in (1, 2, 3):
        slabs.append(shifted(slab, "y", 4 - k))
    for k in range(4):
        slabs.append(shifted(slabs[k], "core", 1))

    query_call = functools.partial(
        call, outs=[((8, 4, 4, 8, queries), f32)], me=me, scratch=[pltpu.VMEM((queries, HALF), bf16)]
    )
    (rot,) = query_call(functools.partial(query_kernel, True), in_specs=[VMEM] + [HELD] * 4, args=(query_grads, *slabs[:4]))
    (rot,) = query_call(
        functools.partial(query_kernel, False),
        in_specs=[VMEM] + [HELD] * 5,
        args=(query_grads, rot, *slabs[4:]),
        held=False,
    )
    rot = exchange(rot, "z")
    rots = call(query_sum_kernel, [((4, 8, queries), f32)] * 4, [HELD], me, args=(rot,))
    rots = [rots[0], *rots[1:]]
    for k in (1, 2, 3):
        rots[k] = shifted(rots[k], "x", k)
    (precond,) = call(
        precond_kernel,
        [((32, 8, 128), f32)],
        [VMEM] + [HELD] * 8,
        me, args=(eigenvalues, *rots, *blocks),
        scratch=[pltpu.VMEM((queries, 128), f32)],
    )
    preconds = [precond]
    for k in (1, 2, 3):
        preconds.append(shifted(precond, "y", k))
    preconds = preconds + [shifted(p, "core", 1) for p in preconds]

    block_shape, sum_shape = ((8, 32, 512), f32), ((2, 512, HALF), bf16)
    sent = [None] * 4
    total_shape = ((4, 128, out_grads.shape[1]), f32)

    def grads_spec(first, stride=0):
        return pl.BlockSpec(
            (512, out_grads.shape[1]), lambda i, me: (lax.rem(me[0] % 4 + 4 - first - stride * i, 4), 0)
        )

    (total,) = call(
        outer_own_kernel,
        [total_shape],
        [SMEM, grads_spec(0), HELD],
        me, args=(doc_lengths, out_grads, blocks[0]), held=False,
    )
    (total,) = call(
        outer_side_kernel,
        [total_shape],
        [SMEM, grads_spec(1, 2), HELD, HELD, VMEM],
        me, args=(doc_lengths, out_grads, blocks[1], blocks[3], total),
        grid=2,
    )
    sent[2], high, low = call(
        train_kernel,
        [block_shape, sum_shape, sum_shape],
        [SMEM, grads_spec(2), *[HELD] * 10],
        me, args=(doc_lengths, out_grads, blocks[2], total, *slabs),
        scratch=[pltpu.VMEM(*total_shape)],
    )
    sent[1], sent[3] = call(
        functools.partial(product_kernel, (1, 3)), [block_shape] * 2, [HELD] * 10, me, args=(high, low, *slabs)
    )
    sent[2] = shifted(sent[2], "x", 2)
    (sent[0],) = call(
        functools.partial(product_kernel, (0,)), [block_shape], [HELD] * 10, me, args=(high, low, *slabs), held=False
    )
    for k in (1, 3):
        sent[k] = shifted(sent[k], "x", k)
    part_spec = pl.BlockSpec((2, 32, 512), lambda i, me: (i, 0, 0))
    (train,) = call(
        train_sum_kernel, [block_shape], [part_spec] * 4, me, args=sent, grid=4, held=False, out_spec=part_spec
    )
    train = exchange(train, "z")

    (partial_scores,) = call(
        score_kernel,
        [((64, 128), f32)],
        [HELD] * 9,
        me, args=(train, *preconds),
        scratch=[pltpu.VMEM((4, 64, 128), f32)],
    )
    return jnp.sum(exchange(partial_scores.reshape(32, 2, 128), ZX), axis=0)[:, :4]


def solution(mesh):
    fine = Mesh(mesh.devices.reshape(4, 2, 8, 4), ("y", "core", "z", "x"))
    seq, factor = ("y", "core"), ("z", "x")
    in_specs = (
        P(seq, factor),
        P(seq, factor),
        P(seq, factor),
        P(seq, factor),
        P(factor, None),
        P(),
        P(factor, None),
        P(seq),
        P(seq),
    )

    return jax.shard_map(local, mesh=fine, in_specs=in_specs, out_specs=P(factor, seq), check_vma=False)
```

```python
import functools

import jax
import jax.numpy as jnp
from jax import lax
from jax.experimental import pallas as pl
from jax.experimental.pallas import tpu as pltpu
from jax.sharding import Mesh, PartitionSpec as P


QLEN = 32
DAMPING = 1.0
ZX = ("z", "x")

PEERS = (1, 3, 2)
HALF = 512
VMEM = pl.BlockSpec(memory_space=pltpu.VMEM)
HELD = pl.BlockSpec(memory_space=pltpu.VMEM)
SMEM = pl.BlockSpec(memory_space=pltpu.SMEM)
ANY = pl.BlockSpec(memory_space=pl.ANY)


def exchange(blocks, axis):
    return lax.all_to_all(blocks, axis, 0, 0, tiled=True)


def shifted(shard, axis, hops):
    n = lax.axis_size(axis)
    return lax.ppermute(shard, axis, [(i, (i + hops) % n) for i in range(n)])


def call(kernel, outs, in_specs, me, *, args, grid=1, scratch=(), held=True):
    out_shape = [(pltpu.VMEM if held else pltpu.HBM)(*o) for o in outs]
    spaces = [pltpu.VMEM if spec is HELD else None if spec is SMEM else pltpu.HBM for spec in in_specs]
    args = [a if space is None else pltpu.with_memory_space_constraint(a, space) for a, space in zip(args, spaces)]
    return pl.pallas_call(
        kernel,
        out_shape=out_shape,
        grid_spec=pltpu.PrefetchScalarGridSpec(
            num_scalar_prefetch=1,
            grid=(grid,),
            in_specs=in_specs,
            out_specs=[VMEM] * len(out_shape),
            scratch_shapes=list(scratch),
        ),
        compiler_params=pltpu.CompilerParams(vmem_limit_bytes=28 << 20),
    )(me, *args)


def place(me_ref):
    me = me_ref[0]
    return me // 64, (me // 32) % 2, (me // 4) % 8, me % 4


def split(value):
    high = value.astype(jnp.bfloat16)
    return high, (value - high.astype(jnp.float32)).astype(jnp.bfloat16)


def dot_nt(left, right):
    return lax.dot_general(
        left, right, (((1,), (1,)), ((), ())), preferred_element_type=jnp.float32
    )


def dot_nn(left, right):
    return lax.dot_general(
        left, right, (((1,), (0,)), ((), ())), preferred_element_type=jnp.float32
    )


def input_rotation_kernel(me_ref, acts_ref, query_ref, basis_ref, *out_refs):
    _, _, _, x = place(me_ref)
    high, low = split(basis_ref[...])
    for k, out_ref in enumerate(out_refs):
        target = lax.rem(x + k, 4)
        acts = acts_ref[pl.ds(pl.multiple_of(target * 512, 512), 512), :]
        query = query_ref[pl.ds(pl.multiple_of(target * 64, 64), 64), :]
        out_ref[:, :64, :] = (dot_nt(acts, high) + dot_nt(acts, low)).reshape(8, 64, 128)
        out_ref[:, 64:, :] = (dot_nt(query, high) + dot_nt(query, low)).reshape(8, 8, 128)


def basis_pick_kernel(me_ref, basis_ref, out_ref, sems):
    y, core, _, _ = place(me_ref)
    cols = basis_ref.shape[1] // 32
    rows = pl.ds(pl.multiple_of(8 * y, 8), 8)
    copies = []
    for f in range(32):
        start = pl.multiple_of(f * cols + core * (cols - HALF), 128)
        copies.append(pltpu.make_async_copy(basis_ref.at[rows, pl.ds(start, HALF)], out_ref.at[f], sems.at[f]))
        copies[-1].start()
    for copy in copies:
        copy.wait()


def query_kernel(own, me_ref, grads_ref, *refs):
    so_far = None if own else refs[0]
    slabs, out_ref, half_ref = refs[-6:-2], refs[-2], refs[-1]
    _, core, _, _ = place(me_ref)
    cols = grads_ref.shape[1]
    half = core if own else 1 - core

    @pl.when(half == 0)
    def _():
        half_ref[...] = grads_ref[:, :HALF]

    @pl.when(half == 1)
    def _():
        half_ref[:, : 2 * HALF - cols] = jnp.zeros((grads_ref.shape[0], 2 * HALF - cols), jnp.bfloat16)
        half_ref[:, 2 * HALF - cols :] = grads_ref[:, HALF:]

    for slot in range(4):
        high, low = split(slabs[slot][...].reshape(256, HALF))
        total = (dot_nt(high, half_ref[...]) + dot_nt(low, half_ref[...])).reshape(8, 4, 8, half_ref.shape[0])
        out_ref[:, :, slot] = total if own else so_far[:, :, slot] + total


def query_sum_kernel(me_ref, blocks_ref, *out_refs):
    _, _, _, x = place(me_ref)
    for k, out_ref in enumerate(out_refs):
        target = lax.rem(x + k, 4)
        total = blocks_ref[0, target]
        for sender in range(1, 8):
            total = total + blocks_ref[sender, target]
        out_ref[...] = total


def precond_kernel(me_ref, eig_ref, *refs):
    parts, blocks, out_ref, rot_in_ref = refs[:4], refs[4:8], refs[8], refs[9]
    y, _, _, x = place(me_ref)
    for k in range(4):
        source = lax.rem(x + 4 - k, 4)
        rot_in_ref[pl.ds(pl.multiple_of(source * 64, 64), 64), :] = blocks[k][:, 64:, :].reshape(64, 128)
    rot = parts[0][...] + parts[1][...] + parts[2][...] + parts[3][...]
    rot = rot.reshape(32, rot.shape[-1])
    lane_query = lax.broadcasted_iota(jnp.int32, rot.shape, 1) // QLEN
    count = rot.shape[1] // QLEN
    masked = jnp.concatenate([jnp.where(lane_query == q, rot, 0.0) for q in range(count)], 0)
    both = lax.dot_general(
        masked,
        rot_in_ref[...],
        (((1,), (0,)), ((), ())),
        precision=lax.Precision.HIGHEST,
        preferred_element_type=jnp.float32,
    ) * (1.0 / QLEN)
    for slot in range(4):
        rows = pl.ds(pl.multiple_of(8 * lax.rem(y + slot, 4), 8), 8)
        eig = eig_ref[rows, :] + DAMPING
        for q in range(count):
            out_ref[rows, q, :] = both[32 * q + 8 * slot : 32 * q + 8 * slot + 8] / eig


def basis_product(me_ref, hops, slabs, high_ref, low_ref, out_ref):
    _, core, _, x = place(me_ref)
    target = lax.rem(x + hops, 4)
    total = None
    for half, group in ((core, slabs[:4]), (1 - core, slabs[4:])):
        value = jnp.concatenate([ref[:, target].reshape(64, HALF) for ref in group], 0)
        high, low = split(value)
        part = dot_nt(high, high_ref[half]) + dot_nt(high, low_ref[half]) + dot_nt(low, high_ref[half])
        total = part if total is None else total + part
    for slot in range(4):
        out_ref[:, 8 * slot : 8 * slot + 8, :] = total[64 * slot : 64 * slot + 64].reshape(8, 8, 512)


def add_block(me_ref, len_ref, hops, grads_ref, block_ref, total_ref):
    _, _, _, x = place(me_ref)
    first = lax.rem(x + 4 - hops, 4) * 512
    high, low = split(block_ref[:, :64, :].reshape(512, 128).T)
    pair = jnp.concatenate([high, low], 0)
    token = first + lax.broadcasted_iota(jnp.int32, pair.shape, 1)
    begin = jnp.int32(0)
    for doc in range(4):
        end = begin + len_ref[doc]

        @pl.when((begin < first + 512) & (end > first))
        def _(begin=begin, end=end, doc=doc):
            masked = jnp.where((token >= begin) & (token < end), pair, jnp.zeros_like(pair))
            both = dot_nn(masked, grads_ref[...])
            total_ref[doc] += both[:128] + both[128:]

        begin = end


def outer_own_kernel(me_ref, len_ref, grads_ref, block_ref, total_ref):
    total_ref[...] = jnp.zeros_like(total_ref)
    add_block(me_ref, len_ref, 0, grads_ref, block_ref, total_ref)


def train_kernel(me_ref, len_ref, grads_ref, *refs):
    blocks, so_far_ref, slabs, (out_ref, high_ref, low_ref, total_ref) = refs[:3], refs[3], refs[4:12], refs[12:]
    cols = grads_ref.shape[1]
    step = pl.program_id(0)

    @pl.when(step == 0)
    def _():
        total_ref[...] = so_far_ref[...]

    for at, hops in enumerate(PEERS):

        @pl.when(step == at)
        def _(at=at, hops=hops):
            add_block(me_ref, len_ref, hops, grads_ref, blocks[at], total_ref)

    @pl.when(step == len(PEERS) - 1)
    def _():
        for doc in range(4):
            length = jnp.full((128, cols), len_ref[doc], jnp.int32).astype(jnp.float32)
            high, low = split(total_ref[doc] / length)
            rows = slice(128 * doc, 128 * doc + 128)
            for ref, value in ((high_ref, high), (low_ref, low)):
                ref[0, rows, :] = value[:, :HALF]
                ref[1, rows, : 2 * HALF - cols] = jnp.zeros((128, 2 * HALF - cols), jnp.bfloat16)
                ref[1, rows, 2 * HALF - cols :] = value[:, HALF:]
        basis_product(me_ref, 2, slabs, high_ref, low_ref, out_ref)


def product_kernel(hops, me_ref, high_ref, low_ref, *refs):
    slabs, out_refs = refs[:8], refs[8:]
    for k, out_ref in zip(hops, out_refs):
        basis_product(me_ref, k, slabs, high_ref, low_ref, out_ref)


def score_kernel(me_ref, blocks_ref, *refs):
    preconds, out_ref, sums_ref = refs[:8], refs[8], refs[9]
    y, core, _, _ = place(me_ref)
    train = blocks_ref[0]
    for sender in range(1, 8):
        train = train + blocks_ref[sender]
    for index, ref in enumerate(preconds):
        other, k = divmod(index, 4)
        owner = 2 * lax.rem(y + 4 - k, 4) + lax.rem(core + other, 2)
        sums = [None] * 4
        for slot in range(4):
            base = 8 * lax.rem(y + slot, 4)
            for r in range(8):
                value = ref[base + r]
                row = train[8 * slot + r : 8 * slot + r + 1]
                for doc in range(4):
                    product = value * row[:, 128 * doc : 128 * doc + 128]
                    sums[doc] = product if sums[doc] is None else sums[doc] + product
        for doc in range(4):
            sums_ref[doc, pl.ds(pl.multiple_of(8 * owner, 8), 8), :] = sums[doc]
    lane = lax.broadcasted_iota(jnp.int32, out_ref.shape, 1)
    scores = jnp.zeros(out_ref.shape, jnp.float32)
    for doc in range(4):
        scores = jnp.where(lane == doc, jnp.sum(sums_ref[doc], axis=1, keepdims=True), scores)
    out_ref[...] = scores


def local(
    out_grads,
    in_acts,
    query_grads,
    query_acts,
    output_basis,
    input_basis,
    eigenvalues,
    doc_ids,
    doc_lengths,
):
    f32, bf16 = jnp.float32, jnp.bfloat16
    me = lax.axis_index(("y", "core", "z", "x")).astype(jnp.int32).reshape(1)
    queries = query_grads.shape[0]

    parts = call(
        input_rotation_kernel,
        [((8, 72, 128), f32)] * 4,
        [VMEM, VMEM, pl.BlockSpec((128, in_acts.shape[1]), lambda i, me: (0, me[0] % 32))],
        me, args=(in_acts, query_acts, input_basis),
    )
    arrived = [parts[0]]
    for k in (2, 1, 3):
        arrived.append(shifted(parts[k], "x", k))
    part = arrived[0] + arrived[1] + arrived[2] + arrived[3]
    part = exchange(part, "z")
    part = jnp.broadcast_to(jnp.sum(part, axis=0)[None], (8, 72, 128))
    block = exchange(part, "z")
    blocks = [block] + [None] * 3
    for k in (2, 1, 3):
        blocks[k] = shifted(block, "x", k)

    (picked,) = call(
        basis_pick_kernel,
        [((32, 8, HALF), f32)],
        [ANY],
        me, args=(output_basis,), held=False,
        scratch=[pltpu.SemaphoreType.DMA((32,))],
    )
    slab = exchange(picked, ZX).reshape(8, 4, 8, HALF)
    slabs = [slab]
    for k in (1, 2, 3):
        slabs.append(shifted(slab, "y", 4 - k))
    for k in range(4):
        slabs.append(shifted(slabs[k], "core", 1))

    query_call = functools.partial(
        call, outs=[((8, 4, 4, 8, queries), f32)], me=me, scratch=[pltpu.VMEM((queries, HALF), bf16)]
    )
    (rot,) = query_call(functools.partial(query_kernel, True), in_specs=[VMEM] + [HELD] * 4, args=(query_grads, *slabs[:4]))
    (rot,) = query_call(
        functools.partial(query_kernel, False),
        in_specs=[VMEM] + [HELD] * 5,
        args=(query_grads, rot, *slabs[4:]),
        held=False,
    )
    rot = exchange(rot, "z")
    rots = call(query_sum_kernel, [((4, 8, queries), f32)] * 4, [HELD], me, args=(rot,))
    rots = [rots[0], *rots[1:]]
    for k in (1, 2, 3):
        rots[k] = shifted(rots[k], "x", k)
    (precond,) = call(
        precond_kernel,
        [((32, 8, 128), f32)],
        [VMEM] + [HELD] * 8,
        me, args=(eigenvalues, *rots, *blocks),
        scratch=[pltpu.VMEM((queries, 128), f32)],
    )
    preconds = [precond]
    for k in (1, 2, 3):
        preconds.append(shifted(precond, "y", k))
    preconds = preconds + [shifted(p, "core", 1) for p in preconds]

    block_shape, sum_shape = ((8, 32, 512), f32), ((2, 512, HALF), bf16)
    sent = [None] * 4
    total_shape = ((4, 128, out_grads.shape[1]), f32)

    def grads_index(step, me):
        return (lax.rem(me[0] % 4 + 4 - jnp.where(step == 2, 2, 1 + 2 * step), 4), 0)

    grads_block = (512, out_grads.shape[1])
    (total,) = call(
        outer_own_kernel,
        [total_shape],
        [SMEM, pl.BlockSpec(grads_block, lambda i, me: (me[0] % 4, 0)), HELD],
        me, args=(doc_lengths, out_grads, blocks[0]),
    )
    sent[2], high, low = call(
        train_kernel,
        [block_shape, sum_shape, sum_shape],
        [SMEM, pl.BlockSpec(grads_block, grads_index), *[HELD] * 12],
        me, args=(doc_lengths, out_grads, *[blocks[k] for k in PEERS], total, *slabs),
        grid=3,
        scratch=[pltpu.VMEM(*total_shape)],
    )
    sent[1], sent[3] = call(
        functools.partial(product_kernel, (1, 3)), [block_shape] * 2, [HELD] * 10, me, args=(high, low, *slabs)
    )
    sent[2] = shifted(sent[2], "x", 2)
    (sent[0],) = call(
        functools.partial(product_kernel, (0,)), [block_shape], [HELD] * 10, me, args=(high, low, *slabs), held=False
    )
    for k in (1, 3):
        sent[k] = shifted(sent[k], "x", k)
    train = sent[0] + sent[1] + sent[2] + sent[3]
    train = exchange(train, "z")

    (partial_scores,) = call(
        score_kernel,
        [((64, 128), f32)],
        [HELD] * 9,
        me, args=(train, *preconds),
        scratch=[pltpu.VMEM((4, 64, 128), f32)],
    )
    return jnp.sum(exchange(partial_scores.reshape(32, 2, 128), ZX), axis=0)[:, :4]


def solution(mesh):
    fine = Mesh(mesh.devices.reshape(4, 2, 8, 4), ("y", "core", "z", "x"))
    seq, factor = ("y", "core"), ("z", "x")
    in_specs = (
        P(seq, factor),
        P(seq, factor),
        P(seq, factor),
        P(seq, factor),
        P(factor, None),
        P(),
        P(factor, None),
        P(seq),
        P(seq),
    )

    return jax.shard_map(local, mesh=fine, in_specs=in_specs, out_specs=P(factor, seq), check_vma=False)
```
